32 devices in a mesh: gx: 8 (over z, y), gy: 4 (over x, core).
Axes of the slice: x: 2, y: 2, z: 4, core: 2. Of those that a mesh axis runs over, the one named last changes fastest.
Arguments:
- rhs: float32 [64, 256, 256], P('gx', 'gy'), may hold values from -12 to 12
- coefs: float32 [13, 64, 256, 256], P(None, 'gx', 'gy'), may hold values from 0 to 1.4, as said below
- shifts: float32 [4], replicated, may hold values from 0.4 to 1.1
Outputs:
- basis: float32 [5, 64, 256, 256], P(None, 'gx', 'gy')
- factor: float32 [5, 5], replicated
- solution: float32 [64, 256, 256], P('gx', 'gy')
- residual: float32 [64, 256, 256], P('gx', 'gy')
The draws below stay inside these ranges and needn't reach their ends.
Inputs may be any that keep to these rules, and one draw needn't show every extreme that they name: `coefs`: entry 0 lies in 0.6 to 1.4, entries 1 to 6 in 0.02 to 0.22, entries 7 to 12 in 0 to 0.16.
All inputs are finite; a program needn't handle non-finite values.
Results may differ from the reference program's by a relative error of at most 0.00095.
Values sent between devices are 32-bit elements; how exact they have to be, the bound alone decides.
A program may use at most 64 MiB of HBM per device.

```python
import jax
import jax.numpy as jnp
from jax import lax

NZ = 256
STEPS = 4
NX = 64
NY = 256


def draw_rhs(key, part):
    noise_key, scale_key = jax.random.split(jax.random.fold_in(key, 11))
    scales = jnp.exp(jax.random.uniform(scale_key, (NX, NY, NZ), jnp.float32, jnp.log(0.1), 0.0))
    plane = jnp.arange(NX, dtype=jnp.float32)
    rising = (1.0 + 2.0 * plane / max(NX - 1, 1))[:, None, None]
    noise = jax.random.truncated_normal(noise_key, -4.0, 4.0, (NX, NY, NZ), jnp.float32)
    return noise * scales * rising


def draw_coefs(key, part):
    lower = jnp.array([0.6] + [0.02] * 6 + [0.0] * 6, jnp.float32)[:, None, None, None]
    upper = jnp.array([1.4] + [0.22] * 6 + [0.16] * 6, jnp.float32)[:, None, None, None]
    unit = jax.random.uniform(jax.random.fold_in(key, 23), (13, NX, NY, NZ), jnp.float32)
    return lower + (upper - lower) * unit


def setup_inputs(seed: int = 0) -> dict:
    splits = jax.random.split(jax.random.key(seed), 4)
    rhs = draw_rhs(jax.random.fold_in(splits[3], 71), 0)
    coefs = draw_coefs(jax.random.fold_in(splits[3], 71), 0)
    shifts = jnp.clip(jax.random.uniform(splits[2], (STEPS,), jnp.float32, 0.4, 1.1), 0.4, 1.1)
    return {"rhs": rhs, "coefs": coefs, "shifts": shifts}


growth = 2.0

def neighbours(field):
    minus_x = jnp.roll(field, 1, axis=0)
    plus_x = jnp.roll(field, -1, axis=0)
    padded = jnp.pad(field, ((0, 0), (1, 1), (1, 1)))
    minus_y = padded[:, :-2, 1:-1]
    plus_y = padded[:, 2:, 1:-1]
    minus_z = padded[:, 1:-1, :-2]
    plus_z = padded[:, 1:-1, 2:]
    return (minus_x, plus_x, minus_y, plus_y, minus_z, plus_z)

def apply_spai(field, coefs):
    total = coefs[0] * field
    near = neighbours(field)
    for index in range(6):
        total = total + coefs[1 + index] * near[index]
    return total

def apply_operator(field, coefs):
    total = field
    near = neighbours(field)
    for index in range(6):
        total = total - coefs[7 + index] * near[index]
    return total

def invert_upper(upper):
    order = upper.shape[0]
    identity = jnp.eye(order, dtype=upper.dtype)
    result = jnp.zeros_like(upper)
    for row in range(order - 1, -1, -1):
        known = identity[row] - jnp.dot(upper[row], result, precision=lax.Precision.HIGHEST)
        result = result.at[row].set(known / upper[row, row])
    return result

def least_squares(factor, shifts):
    count = shifts.shape[0]
    relation = jnp.zeros((count + 1, count), jnp.float32)
    for column in range(count):
        relation = relation.at[column, column].set(shifts[column])
        relation = relation.at[column + 1, column].set(1.0 / growth)
    hessenberg = jnp.dot(factor, relation, precision=lax.Precision.HIGHEST)
    target = factor[:, 0]
    for column in range(count):
        top = hessenberg[column]
        below = hessenberg[column + 1]
        radius = jnp.sqrt(top[column] ** 2 + below[column] ** 2)
        cosine = top[column] / radius
        sine = below[column] / radius
        hessenberg = hessenberg.at[column].set(cosine * top + sine * below)
        hessenberg = hessenberg.at[column + 1].set(cosine * below - sine * top)
        first_entry = target[column]
        second_entry = target[column + 1]
        target = target.at[column].set(cosine * first_entry + sine * second_entry)
        target = target.at[column + 1].set(cosine * second_entry - sine * first_entry)
    upper = hessenberg[:count]
    weights = jnp.dot(invert_upper(upper), target[:count], precision=lax.Precision.HIGHEST)
    combine = -jnp.dot(relation, weights, precision=lax.Precision.HIGHEST)
    combine = combine.at[0].add(1.0)
    return (weights, combine)

def reference(rhs, coefs, shifts):
    count = shifts.shape[0]
    basis_list = [rhs]
    images = []
    for step in range(count):
        image = apply_spai(basis_list[step], coefs)
        images.append(image)
        applied = apply_operator(image, coefs)
        basis_list.append(growth * (applied - shifts[step] * basis_list[step]))
    stacked = jnp.stack(basis_list)
    flat = stacked.reshape(count + 1, -1)
    gram = jnp.dot(flat, flat.T, precision=lax.Precision.HIGHEST) / flat.shape[1]
    factor = jnp.linalg.cholesky(gram).T
    inverse = invert_upper(factor)
    ortho = jnp.dot(inverse.T, flat, precision=lax.Precision.HIGHEST).reshape(stacked.shape)
    weights, combine = least_squares(factor, shifts)
    image_flat = jnp.stack(images).reshape(count, -1)
    solution = jnp.dot(weights, image_flat, precision=lax.Precision.HIGHEST).reshape(rhs.shape)
    residual = jnp.dot(combine, flat, precision=lax.Precision.HIGHEST).reshape(rhs.shape)
    return (ortho, factor, solution, residual)
```

```python
import functools

import jax
import jax.numpy as jnp
from jax import lax
from jax.experimental import pallas as pl
from jax.experimental.pallas import tpu as pltpu
from jax.sharding import PartitionSpec as P

growth = 2.0
MESH = pl.DeviceIdType.MESH
PAD = 8
ROWS = 128
TILE = 8


def middle_out(count):
    low, high = (count - 1) // 2, (count - 1) // 2 + 1
    order = []
    while low >= 0 or high < count:
        if high < count:
            order.append(high)
            high += 1
        if low >= 0:
            order.append(low)
            low -= 1
    return order


def basis_kernel(
    n_gx, n_gy, shifts_hbm, rhs, coefs, fv, fw, gram,
    weight, part, peers, shifts, xout, xin, yout, yin, cout, cin,
    far, far_corner, own_row, own_corner, near_row, near_corner, far_edge,
    load_sem, xs, xr, ys, yr, cs, cr, fs, fr, gs, gr,
):
    steps = shifts.shape[0]
    order = steps + 1
    nx, ny, nz = rhs.shape
    tiles = ny // TILE
    body = slice(PAD, PAD + ny)
    face = (0, nx - 1)
    edge = (0, ny - 1)
    gx, gy = lax.axis_index("gx"), lax.axis_index("gy")
    beside_x = (lax.rem(gx + n_gx - 1, n_gx), lax.rem(gx + 1, n_gx))
    beside_y = (jnp.maximum(gy - 1, 0), jnp.minimum(gy + 1, n_gy - 1))
    there = (gy > 0, gy < n_gy - 1)
    count = n_gx * n_gy
    me = gx * n_gy + gy

    loads = [
        pltpu.make_async_copy(rhs, fv.at[0, :, body, :], load_sem.at[0]),
        pltpu.make_async_copy(coefs.at[0:7], weight.at[0:7], load_sem.at[1]),
        pltpu.make_async_copy(coefs.at[7:13], weight.at[7:13], load_sem.at[2]),
        pltpu.make_async_copy(shifts_hbm, shifts, load_sem.at[3]),
    ]
    for load in loads:
        load.start()

    cin[...] = jnp.zeros_like(cin)

    barrier = pltpu.get_barrier_semaphore()

    def peer(d):
        other = lax.rem(me + d, count)
        return {"gx": lax.div(other, n_gy), "gy": lax.rem(other, n_gy)}

    def greet(d, c):
        pl.semaphore_signal(barrier, inc=1, device_id=peer(d), device_id_type=MESH)
        return c

    lax.fori_loop(1, count, greet, 0)

    part[...] = jnp.zeros_like(part)
    blank = jnp.zeros((PAD, nz), jnp.float32)
    for fields in (fv, fw):

        def clear(p, c):
            for k in range(fields.shape[0]):
                fields[k, p, 0:PAD, :] = blank
                fields[k, p, PAD + ny : PAD + ny + PAD, :] = blank
            return c

        lax.fori_loop(0, nx, clear, 0)

    def rows_of(t):
        return slice(t * TILE, (t + 1) * TILE)

    def remote(source, target, send, receive, device):
        return pltpu.make_async_remote_copy(
            src_ref=source, dst_ref=target, send_sem=send, recv_sem=receive,
            device_id=device, device_id_type=MESH,
        )

    def x_copy(k, s, t):
        n, m = (2 * k + s) * tiles + t, (2 * k + 1 - s) * tiles + t
        return remote(
            xout.at[k, s, :, rows_of(t), :], xin.at[k, 1 - s, :, rows_of(t), :],
            xs.at[n], xr.at[m], {"gx": beside_x[s]},
        )

    def y_copy(k, s):
        return remote(
            yout.at[k, s], yin.at[k, 1 - s], ys.at[2 * k + s], yr.at[2 * k + 1 - s], {"gy": beside_y[s]}
        )

    def corner_copy(k, sx, sy):
        n, m = 4 * k + 2 * sx + sy, 4 * k + 2 * (1 - sx) + 1 - sy
        return remote(
            cout.at[n], cin.at[m], cs.at[n], cr.at[m], {"gx": beside_x[sx], "gy": beside_y[sy]}
        )

    def far_copy(s, t):
        return remote(
            weight.at[1 + s, face[s], rows_of(t), :], far.at[1 - s, rows_of(t), :],
            fs.at[s, t], fr.at[1 - s, t], {"gx": beside_x[s]},
        )

    def far_edge_copy(s):
        return remote(
            far_corner.at[s], far_edge.at[1 - s], fs.at[s, tiles], fr.at[1 - s, tiles], {"gx": beside_x[s]}
        )

    def near_copies(s):
        device = {"gy": beside_y[s]}
        return (
            remote(own_row.at[s], near_row.at[1 - s], fs.at[s, tiles + 1], fr.at[1 - s, tiles + 1], device),
            remote(own_corner.at[s], near_corner.at[1 - s], fs.at[s, tiles + 2], fr.at[1 - s, tiles + 2], device),
        )

    def along_z(centre):
        lane = lax.broadcasted_iota(jnp.int32, centre.shape, 1)
        return (
            jnp.where(lane == 0, 0.0, pltpu.roll(centre, 1, 1)),
            jnp.where(lane == nz - 1, 0.0, pltpu.roll(centre, nz - 1, 1)),
        )

    def block_m(k, p, r, rows, low=True, high=True):
        here = slice(PAD + r, PAD + r + rows)
        mine = slice(r, r + rows)
        centre = fv[k, p, here, :]
        total = weight[0, p, mine, :] * centre
        if low:
            total = total + weight[1, p, mine, :] * fv[k, p - 1, here, :]
        if high:
            total = total + weight[2, p, mine, :] * fv[k, p + 1, here, :]
        total = total + weight[3, p, mine, :] * fv[k, p, PAD + r - 1 : PAD + r - 1 + rows, :]
        total = total + weight[4, p, mine, :] * fv[k, p, PAD + r + 1 : PAD + r + 1 + rows, :]
        minus_z, plus_z = along_z(centre)
        total = total + weight[5, p, mine, :] * minus_z
        total = total + weight[6, p, mine, :] * plus_z
        fw[k, p, here, :] = total
        return total

    def block_a(k, p, r, rows, minus_x=None, plus_x=None):
        here = slice(PAD + r, PAD + r + rows)
        mine = slice(r, r + rows)
        centre = fw[k, p, here, :]
        if minus_x is None:
            minus_x = fw[k, p - 1, here, :]
        if plus_x is None:
            plus_x = fw[k, p + 1, here, :]
        total = centre - weight[7, p, mine, :] * minus_x
        total = total - weight[8, p, mine, :] * plus_x
        total = total - weight[9, p, mine, :] * fw[k, p, PAD + r - 1 : PAD + r - 1 + rows, :]
        total = total - weight[10, p, mine, :] * fw[k, p, PAD + r + 1 : PAD + r + 1 + rows, :]
        minus_z, plus_z = along_z(centre)
        total = total - weight[11, p, mine, :] * minus_z
        total = total - weight[12, p, mine, :] * plus_z
        total = growth * (total - shifts[k] * fv[k, p, here, :])
        fv[k + 1, p, here, :] = total
        return total

    def face_m(k, s, t):
        total = block_m(k, face[s], t * TILE, TILE, low=s == 1, high=s == 0)
        xout[k, s, 1, rows_of(t), :] = total

    def face_a(k, s, t):
        rows = rows_of(t)
        here = slice(PAD + t * TILE, PAD + (t + 1) * TILE)
        beyond = xin[k, s, 1, rows, :] + far[s, rows, :] * fv[k, face[s], here, :]
        if s == 0:
            total = block_a(k, 0, t * TILE, TILE, minus_x=beyond)
        else:
            total = block_a(k, nx - 1, t * TILE, TILE, plus_x=beyond)
        xout[k + 1, s, 0, rows, :] = total

    def send_corners(k):
        for sy in range(2):
            for sx in range(2):
                row = PAD + edge[sy]
                cout[4 * k + 2 * sx + sy, :, :] = fv[k, face[sx], row : row + 1, :]

            @pl.when(there[sy])
            def _():
                for sx in range(2):
                    corner_copy(k, sx, sy).start()

    def send_y(k):
        for s in range(2):
            row = PAD + edge[s]

            @pl.when(there[s])
            def _():
                for p in range(nx):
                    yout[k, s, 0, p : p + 1, :] = fv[k, p, row : row + 1, :]
                    yout[k, s, 1, p : p + 1, :] = fw[k, p, row : row + 1, :]
                y_copy(k, s).start()

    def finish_edges(k):
        for sy in range(2):

            @pl.when(there[sy])
            def _():
                for sx in range(2):
                    corner_copy(k, 1 - sx, 1 - sy).wait_recv()
                y_copy(k, 1 - sy).wait_recv()
                row = PAD + edge[sy]
                halo = PAD - 1 if sy == 0 else PAD + ny
                yin[k, sy, 1, :, :] = yin[k, sy, 1, :, :] + near_row[sy] * yout[k, sy, 0, :, :]
                yin[k, sy, 0, :, :] = own_row[sy] * yin[k, sy, 0, :, :]
                for sx in range(2):
                    p, q = face[sx], edge[sy]
                    line = cin[4 * k + 2 * sx + sy, :, :]
                    yin[k, sy, 1, p : p + 1, :] = yin[k, sy, 1, p : p + 1, :] + near_corner[sy, sx : sx + 1, :] * line
                    xin[k, sx, 1, q : q + 1, :] = xin[k, sx, 1, q : q + 1, :] + far_edge[sx, sy : sy + 1, :] * line
                for p in range(nx):
                    fw[k, p, halo : halo + 1, :] = yin[k, sy, 1, p : p + 1, :]
                    fw[k, p, row : row + 1, :] = fw[k, p, row : row + 1, :] + yin[k, sy, 0, p : p + 1, :]

    def products(i):
        def one(j, c):
            def add(p, total):
                a = fv[i, p, body, :]
                b = fv[j, p, body, :]
                return total + jnp.sum((a * b).reshape(ny // 8, 8, nz), axis=0)

            keep(i * (i + 1) // 2 + j, lax.fori_loop(0, nx, add, jnp.zeros((8, nz), jnp.float32)))
            return c

        lax.fori_loop(0, i + 1, one, 0)

    def keep(n, total):
        row = jnp.sum(total, axis=0, keepdims=True)
        flat = row[:, :ROWS]
        for q in range(1, nz // ROWS):
            flat = flat + row[:, q * ROWS : (q + 1) * ROWS]
        part[pl.ds(n, 1), :] = flat

    def last_products():
        def add(p, totals):
            a = fv[steps, p, body, :]
            return tuple(
                total + jnp.sum((a * fv[j, p, body, :]).reshape(ny // 8, 8, nz), axis=0)
                for j, total in enumerate(totals)
            )

        totals = lax.fori_loop(0, nx, add, tuple(jnp.zeros((8, nz), jnp.float32) for _ in range(order)))
        for j, total in enumerate(totals):
            keep(steps * (steps + 1) // 2 + j, total)

    def inner_rows():
        return [(r, min(16, ny - TILE - r)) for r in range(TILE, ny - TILE, 16)]

    def inner_m(k):
        def one(p, c):
            for r, rows in inner_rows():
                block_m(k, p, r, rows)
            return c

        lax.fori_loop(1, nx - 1, one, 0)

    def inner_a(k):
        def one(p, c):
            for r, rows in inner_rows():
                block_a(k, p, r, rows)
            return c

        lax.fori_loop(2, nx - 2, one, 0)

    def edge_m(k):
        def one(p, c):
            block_m(k, p, 0, TILE)
            block_m(k, p, ny - TILE, TILE)
            return c

        lax.fori_loop(1, nx - 1, one, 0)

    def edge_a(k):
        def one(p, c):
            block_a(k, p, 0, TILE)
            block_a(k, p, ny - TILE, TILE)
            return c

        lax.fori_loop(2, nx - 2, one, 0)

    sequence = middle_out(tiles)

    loads[0].wait()
    for s in range(2):
        xout[0, s, 0, :, :] = fv[0, face[s], body, :]
    loads[1].wait()
    for t in sequence:
        for s in range(2):
            face_m(0, s, t)
    edge_m(0)
    for s in range(2):
        r = edge[s]
        for p in range(nx):
            own_row[s, p : p + 1, :] = weight[3 + s, p, r : r + 1, :]
        for sx in range(2):
            own_corner[s, sx : sx + 1, :] = weight[1 + sx, face[sx], r : r + 1, :]
        for sy in range(2):
            far_corner[s, sy : sy + 1, :] = weight[3 + sy, face[s], edge[sy] : edge[sy] + 1, :]
    pl.semaphore_wait(barrier, count - 1)
    for s in range(2):
        far_edge_copy(s).start()
    send_corners(0)
    for t in sequence:
        for s in range(2):
            x_copy(0, s, t).start()
            far_copy(s, t).start()
    for s in range(2):

        @pl.when(there[s])
        def _():
            for copy in near_copies(s):
                copy.start()

    send_y(0)
    inner_m(0)
    loads[2].wait()
    loads[3].wait()

    def step(k, send):
        inner_a(k)
        products(k)
        arrived, final, drafted = set(), set(), set()

        def needs(u):
            return {q for q in (u - 1, u, u + 1) if 0 <= q < tiles}

        for t in sequence:
            for s in range(2):
                x_copy(k, 1 - s, t).wait_recv()

                @pl.when(k == 0)
                def _():
                    far_copy(1 - s, t).wait_recv()

                here = slice(PAD + t * TILE, PAD + (t + 1) * TILE)
                fw[k, face[s], here, :] = (
                    fw[k, face[s], here, :] + weight[1 + s, face[s], rows_of(t), :] * xin[k, s, 0, rows_of(t), :]
                )
            arrived.add(t)
            last = len(arrived) == tiles
            if last:

                @pl.when(k == 0)
                def _():
                    for s in range(2):
                        far_edge_copy(1 - s).wait_recv()

                        @pl.when(there[s])
                        def _():
                            for copy in near_copies(1 - s):
                                copy.wait_recv()

                finish_edges(k)
            ready = [
                u for u in sequence
                if u not in final and needs(u) <= arrived and (last or 0 < u < tiles - 1)
            ]
            for u in ready:
                final.add(u)
            extra = sorted(set().union(*[needs(u) for u in ready]) - final) if send and ready else []
            for u in ready + extra:
                for s in range(2):
                    face_a(k, s, u)
            for u in ready:
                block_a(k, 1, u * TILE, TILE)
                block_a(k, nx - 2, u * TILE, TILE)
            if send:
                if last:
                    send_corners(k + 1)
                for u in ready:
                    for s in range(2):
                        face_m(k + 1, s, u)
                        x_copy(k + 1, s, u).start()
        edge_a(k)
        if send:
            edge_m(k + 1)
            send_y(k + 1)
            inner_m(k + 1)

    def looped(k, c):
        step(k, True)
        return c

    lax.fori_loop(0, steps - 1, looped, 0)
    step(steps - 1, False)
    last_products()

    height = part.shape[0]
    row = lax.broadcasted_iota(jnp.int32, (height, ROWS), 0)
    lane = lax.broadcasted_iota(jnp.int32, (height, ROWS), 1)
    sums = jnp.sum(part[...], axis=1, keepdims=True)
    packed = jnp.sum(jnp.where(row == lane, jnp.broadcast_to(sums, row.shape), 0.0), axis=0, keepdims=True)
    peers[pl.ds(me, 1), :] = packed

    def peer_copy(d):
        return remote(peers.at[pl.ds(me, 1), :], peers.at[pl.ds(me, 1), :], gs.at[d], gr.at[d], peer(d))

    def peer_start(d, c):
        peer_copy(d).start()
        return c

    def peer_arrive(d, c):
        peer_copy(d).wait_recv()
        return c

    def peer_sent(d, c):
        peer_copy(d).wait_send()
        return c

    lax.fori_loop(1, count, peer_start, 0)

    def sent(k, c):
        for s in range(2):
            for t in range(tiles):
                x_copy(k, s, t).wait_send()

            @pl.when(there[s])
            def _():
                y_copy(k, s).wait_send()
                for sx in range(2):
                    corner_copy(k, sx, s).wait_send()

        return c

    lax.fori_loop(0, steps, sent, 0)
    for s in range(2):
        for t in range(tiles):
            far_copy(s, t).wait_send()
        far_edge_copy(s).wait_send()

        @pl.when(there[s])
        def _():
            for copy in near_copies(s):
                copy.wait_send()

    lax.fori_loop(1, count, peer_arrive, 0)
    total = jnp.sum(peers[...], axis=0, keepdims=True)
    spread = jnp.sum(jnp.where(row == lane, jnp.broadcast_to(total, row.shape), 0.0), axis=1, keepdims=True)
    gram[0:height, :] = jnp.broadcast_to(spread, row.shape)
    for k in range(steps):
        gram[height + k : height + k + 1, :] = jnp.full((1, ROWS), shifts[k], jnp.float32)
    lax.fori_loop(1, count, peer_sent, 0)


def small_algebra(gram, steps, cells):
    order = steps + 1
    height = -(-(order * (order + 1) // 2) // 8) * 8
    shifts = [gram[height + k : height + k + 1, :] for k in range(steps)]
    sums = gram[:height] / cells

    def entry(i, j):
        n = max(i, j) * (max(i, j) + 1) // 2 + min(i, j)
        return sums[n : n + 1, :]

    factor = {}
    for i in range(order):
        value = entry(i, i)
        for k in range(i):
            value = value - factor[k, i] * factor[k, i]
        factor[i, i] = jnp.sqrt(value)
        for j in range(i + 1, order):
            value = entry(i, j)
            for k in range(i):
                value = value - factor[k, i] * factor[k, j]
            factor[i, j] = value / factor[i, i]
    inverse = {}
    for j in range(order):
        inverse[j, j] = 1.0 / factor[j, j]
        for i in range(j - 1, -1, -1):
            value = factor[i, i + 1] * inverse[i + 1, j]
            for k in range(i + 2, j + 1):
                value = value + factor[i, k] * inverse[k, j]
            inverse[i, j] = -value / factor[i, i]
    zero = jnp.zeros_like(factor[0, 0])

    def upper(i, j):
        return factor.get((i, j), zero)

    hess = [[upper(i, k) * shifts[k] + upper(i, k + 1) * (1.0 / growth) for k in range(steps)] for i in range(order)]
    target = [upper(i, 0) for i in range(order)]
    for k in range(steps):
        top, below = hess[k][k], hess[k + 1][k]
        radius = jnp.sqrt(top * top + below * below)
        cosine, sine = top / radius, below / radius
        for c in range(k, steps):
            a, b = hess[k][c], hess[k + 1][c]
            hess[k][c] = cosine * a + sine * b
            hess[k + 1][c] = cosine * b - sine * a
        a, b = target[k], target[k + 1]
        target[k] = cosine * a + sine * b
        target[k + 1] = cosine * b - sine * a
    weights = [None] * steps
    for i in range(steps - 1, -1, -1):
        value = target[i]
        for k in range(i + 1, steps):
            value = value - hess[i][k] * weights[k]
        weights[i] = value / hess[i][i]
    combine = []
    for j in range(order):
        value = zero + (1.0 if j == 0 else 0.0)
        if j < steps:
            value = value - shifts[j] * weights[j]
        if j > 0:
            value = value - (1.0 / growth) * weights[j - 1]
        combine.append(value)
    return factor, inverse, weights, combine


def combine_kernel(cells, gram, v, w, basis, factor_out, solution_out, residual, table, basis_v, sol_v, res_v, sem):
    order, nx, ny, nz = basis_v.shape
    steps = order - 1
    pairs = [(j, k) for k in range(order) for j in range(k + 1)]
    tail = len(pairs)

    factor, inverse, weights, combine = small_algebra(gram[...], steps, cells)
    values = [inverse[p] for p in pairs] + weights + combine
    for n, value in enumerate(values):
        table[n] = jnp.broadcast_to(value, table.shape[1:])
    row = lax.broadcasted_iota(jnp.int32, (8, ROWS), 0)
    column = lax.broadcasted_iota(jnp.int32, (8, ROWS), 1)
    whole = jnp.zeros((8, ROWS), jnp.float32)
    for (i, j), value in factor.items():
        whole = jnp.where((row == i) & (column == j), value, whole)
    factor_out[...] = whole[:order, :order]

    def mul(n, x):
        return table[n][None] * x

    deep = 16 if ny % 16 == 0 else 8

    def tile(p, t):
        rows = pl.ds(pl.multiple_of(t * deep, deep), deep)
        for q in range(0, nz, ROWS):
            lanes = slice(q, q + ROWS)
            load = lambda x: x.reshape(deep // 8, 8, ROWS)
            padded = pl.ds(pl.multiple_of(PAD + t * deep, 8), deep)
            fields = [load(v[k, p, padded, lanes]) for k in range(order)]
            for k in range(order):
                total = None
                for j in range(k + 1):
                    term = mul(pairs.index((j, k)), fields[j])
                    total = term if total is None else total + term
                basis_v[k, p, rows, lanes] = total.reshape(deep, ROWS)
            total = mul(tail, load(w[0, p, padded, lanes]))
            for k in range(1, steps):
                total = total + mul(tail + k, load(w[k, p, padded, lanes]))
            sol_v[p, rows, lanes] = total.reshape(deep, ROWS)
            total = mul(tail + steps, fields[0])
            for j in range(1, order):
                total = total + mul(tail + steps + j, fields[j])
            res_v[p, rows, lanes] = total.reshape(deep, ROWS)

    def copies(p):
        return (
            pltpu.make_async_copy(basis_v.at[:, p], basis.at[:, p], sem.at[p, 0]),
            pltpu.make_async_copy(sol_v.at[p], solution_out.at[p], sem.at[p, 1]),
            pltpu.make_async_copy(res_v.at[p], residual.at[p], sem.at[p, 2]),
        )

    def plane(p, c):
        def inner(t, d):
            tile(p, t)
            return d

        lax.fori_loop(0, ny // deep, inner, 0)
        for copy in copies(p):
            copy.start()
        return c

    def finish(p, c):
        for copy in copies(p):
            copy.wait()
        return c

    lax.fori_loop(0, nx, plane, 0)
    lax.fori_loop(0, nx, finish, 0)


def device_body(n_gx, n_gy, rhs, coefs, shifts):
    steps = shifts.shape[0]
    order = steps + 1
    nx, ny, nz = rhs.shape
    f32 = jnp.float32
    grown = (nx, ny + 2 * PAD, nz)
    height = -(-(order * (order + 1) // 2) // 8) * 8
    gram_rows = height + -(-steps // 8) * 8
    tiles = ny // TILE
    hbm = pl.BlockSpec(memory_space=pltpu.HBM)
    vmem = pl.BlockSpec(memory_space=pltpu.VMEM)
    dma = pltpu.SemaphoreType.DMA
    rhs = pltpu.with_memory_space_constraint(rhs, pltpu.HBM)
    coefs = pltpu.with_memory_space_constraint(coefs, pltpu.HBM)
    shifts = pltpu.with_memory_space_constraint(shifts, pltpu.HBM)
    v, w, gram = pl.pallas_call(
        functools.partial(basis_kernel, n_gx, n_gy),
        out_shape=(
            jax.ShapeDtypeStruct((order,) + grown, f32),
            jax.ShapeDtypeStruct((steps,) + grown, f32),
            jax.ShapeDtypeStruct((gram_rows, ROWS), f32),
        ),
        in_specs=[hbm, hbm, hbm],
        out_specs=(vmem, vmem, vmem),
        scratch_shapes=[
            pltpu.VMEM(coefs.shape, f32),
            pltpu.VMEM((height, ROWS), f32),
            pltpu.VMEM((n_gx * n_gy, ROWS), f32),
            pltpu.SMEM(shifts.shape, f32),
            pltpu.VMEM((order, 2, 2, ny, nz), f32),
            pltpu.VMEM((steps, 2, 2, ny, nz), f32),
            pltpu.VMEM((order, 2, 2, nx, nz), f32),
            pltpu.VMEM((steps, 2, 2, nx, nz), f32),
            pltpu.VMEM((4 * order, 1, nz), f32),
            pltpu.VMEM((4 * steps, 1, nz), f32),
            pltpu.VMEM((2, ny, nz), f32),
            pltpu.VMEM((2, 2, nz), f32),
            pltpu.VMEM((2, nx, nz), f32),
            pltpu.VMEM((2, 2, nz), f32),
            pltpu.VMEM((2, nx, nz), f32),
            pltpu.VMEM((2, 2, nz), f32),
            pltpu.VMEM((2, 2, nz), f32),
            dma((4,)),
            dma((2 * steps * tiles,)),
            dma((2 * steps * tiles,)),
            dma((2 * steps,)),
            dma((2 * steps,)),
            dma((4 * steps,)),
            dma((4 * steps,)),
            dma((2, tiles + 3)),
            dma((2, tiles + 3)),
            dma((n_gx * n_gy,)),
            dma((n_gx * n_gy,)),
        ],
        compiler_params=pltpu.CompilerParams(
            collective_id=0, has_side_effects=True, vmem_limit_bytes=32 * 2**20
        ),
        name="basis",
    )(shifts, rhs, coefs)

    cells = float(nx * ny * nz * n_gx * n_gy)
    return pl.pallas_call(
        functools.partial(combine_kernel, cells),
        out_shape=(
            jax.ShapeDtypeStruct((order, nx, ny, nz), f32),
            jax.ShapeDtypeStruct((order, order), f32),
            jax.ShapeDtypeStruct((nx, ny, nz), f32),
            jax.ShapeDtypeStruct((nx, ny, nz), f32),
        ),
        in_specs=[vmem, vmem, vmem],
        out_specs=(hbm, vmem, hbm, hbm),
        scratch_shapes=[
            pltpu.VMEM((order * (order + 1) // 2 + steps + order, 8, ROWS), f32),
            pltpu.VMEM((order, nx, ny, nz), f32),
            pltpu.VMEM((nx, ny, nz), f32),
            pltpu.VMEM((nx, ny, nz), f32),
            dma((nx, 3)),
        ],
        compiler_params=pltpu.CompilerParams(vmem_limit_bytes=32 * 2**20),
        name="combine",
    )(gram, v, w)


def solution(mesh):
    placed = (P("gx", "gy", None), P(None, "gx", "gy", None), P())
    return jax.shard_map(
        functools.partial(device_body, mesh.shape["gx"], mesh.shape["gy"]),
        mesh=mesh,
        in_specs=placed,
        out_specs=(P(None, "gx", "gy", None), P(), P("gx", "gy", None), P("gx", "gy", None)),
        check_vma=False,
    )
```

```python
import functools

import jax
import jax.numpy as jnp
from jax import lax
from jax.experimental import pallas as pl
from jax.experimental.pallas import tpu as pltpu
from jax.sharding import PartitionSpec as P

growth = 2.0
MESH = pl.DeviceIdType.MESH
PAD = 8
ROWS = 128
TILE = 8


def middle_out(count):
    low, high = (count - 1) // 2, (count - 1) // 2 + 1
    order = []
    while low >= 0 or high < count:
        if high < count:
            order.append(high)
            high += 1
        if low >= 0:
            order.append(low)
            low -= 1
    return order


def basis_kernel(
    n_gx, n_gy, shifts_hbm, rhs, coefs, fv, fw, gram,
    weight, part, sums, peers, shifts, xout, xin, yout, yin, cout, cin,
    far, far_corner, own_row, own_corner, near_row, near_corner, far_edge,
    load_sem, hello, xs, xr, ys, yr, cs, cr, fs, fr, gs, gr,
):
    steps = shifts.shape[0]
    order = steps + 1
    nx, ny, nz = rhs.shape
    tiles = ny // TILE
    body = slice(PAD, PAD + ny)
    face = (0, nx - 1)
    edge = (0, ny - 1)
    gx, gy = lax.axis_index("gx"), lax.axis_index("gy")
    beside_x = (lax.rem(gx + n_gx - 1, n_gx), lax.rem(gx + 1, n_gx))
    beside_y = (jnp.maximum(gy - 1, 0), jnp.minimum(gy + 1, n_gy - 1))
    there = (gy > 0, gy < n_gy - 1)
    count = n_gx * n_gy
    me = gx * n_gy + gy

    loads = [
        pltpu.make_async_copy(rhs, fv.at[0, :, body, :], load_sem.at[0]),
        pltpu.make_async_copy(coefs.at[0:7, 0], weight.at[0:7, 0], load_sem.at[1]),
        pltpu.make_async_copy(coefs.at[0:7, nx - 1], weight.at[0:7, nx - 1], load_sem.at[2]),
        pltpu.make_async_copy(coefs.at[0:7, 1 : nx - 1], weight.at[0:7, 1 : nx - 1], load_sem.at[3]),
        pltpu.make_async_copy(coefs.at[7:13], weight.at[7:13], load_sem.at[4]),
        pltpu.make_async_copy(shifts_hbm, shifts, load_sem.at[5]),
    ]
    for load in loads:
        load.start()

    cin[...] = jnp.zeros_like(cin)

    barrier = pltpu.get_barrier_semaphore()

    def peer(d):
        other = lax.rem(me + d, count)
        return {"gx": lax.div(other, n_gy), "gy": lax.rem(other, n_gy)}

    def greet(device):
        pl.semaphore_signal(barrier, inc=1, device_id=device, device_id_type=MESH)

    for x in beside_x:
        greet({"gx": x})
    for s in range(2):

        @pl.when(there[s])
        def _():
            greet({"gy": beside_y[s]})
            for x in beside_x:
                greet({"gx": x, "gy": beside_y[s]})

    greet(peer(1))
    greet(peer(count - 1))
    greetings = 4 + 3 * (there[0].astype(jnp.int32) + there[1].astype(jnp.int32))

    strides = []
    while (2 ** len(strides)) * 2 < count:
        strides.append(2 ** len(strides))

    def hello_signal(r):
        for d in (strides[r], count - strides[r]):
            pl.semaphore_signal(hello.at[r], inc=1, device_id=peer(d), device_id_type=MESH)

    def hello_rounds(k):
        share = -(-len(strides) // steps)
        for r in range(k * share, min((k + 1) * share, len(strides))):
            pl.semaphore_wait(hello.at[r], 2)
            if r + 1 < len(strides):
                hello_signal(r + 1)

    part[...] = jnp.zeros_like(part)
    blank = jnp.zeros((PAD, nz), jnp.float32)
    for fields in (fv, fw):

        def clear(p, c):
            for k in range(fields.shape[0]):
                fields[k, p, 0:PAD, :] = blank
                fields[k, p, PAD + ny : PAD + ny + PAD, :] = blank
            return c

        lax.fori_loop(0, nx, clear, 0)

    def rows_of(t):
        return slice(t * TILE, (t + 1) * TILE)

    def remote(source, target, send, receive, device):
        return pltpu.make_async_remote_copy(
            src_ref=source, dst_ref=target, send_sem=send, recv_sem=receive,
            device_id=device, device_id_type=MESH,
        )

    def x_copy(k, s, t):
        n, m = (2 * k + s) * tiles + t, (2 * k + 1 - s) * tiles + t
        kinds = slice(1 if k == 0 else 0, 2)
        return remote(
            xout.at[k, s, kinds, rows_of(t), :], xin.at[k, 1 - s, kinds, rows_of(t), :],
            xs.at[n], xr.at[m], {"gx": beside_x[s]},
        )

    def y_copy(k, s):
        return remote(
            yout.at[k, s], yin.at[k, 1 - s], ys.at[2 * k + s], yr.at[2 * k + 1 - s], {"gy": beside_y[s]}
        )

    def corner_copy(k, sx, sy):
        n, m = 4 * k + 2 * sx + sy, 4 * k + 2 * (1 - sx) + 1 - sy
        return remote(
            cout.at[n], cin.at[m], cs.at[n], cr.at[m], {"gx": beside_x[sx], "gy": beside_y[sy]}
        )

    def first_copy(s):
        return remote(
            rhs.at[face[s]], xin.at[0, 1 - s, 0], fs.at[s, tiles + 3], fr.at[1 - s, tiles + 3], {"gx": beside_x[s]}
        )

    def far_copy(s, t):
        return remote(
            coefs.at[1 + s, face[s], rows_of(t), :], far.at[1 - s, rows_of(t), :],
            fs.at[s, t], fr.at[1 - s, t], {"gx": beside_x[s]},
        )

    def far_edge_copy(s):
        return remote(
            far_corner.at[s], far_edge.at[1 - s], fs.at[s, tiles], fr.at[1 - s, tiles], {"gx": beside_x[s]}
        )

    def near_copies(s):
        device = {"gy": beside_y[s]}
        return (
            remote(own_row.at[s], near_row.at[1 - s], fs.at[s, tiles + 1], fr.at[1 - s, tiles + 1], device),
            remote(own_corner.at[s], near_corner.at[1 - s], fs.at[s, tiles + 2], fr.at[1 - s, tiles + 2], device),
        )

    def along_z(centre):
        lane = lax.broadcasted_iota(jnp.int32, centre.shape, 1)
        return (
            jnp.where(lane == 0, 0.0, pltpu.roll(centre, 1, 1)),
            jnp.where(lane == nz - 1, 0.0, pltpu.roll(centre, nz - 1, 1)),
        )

    def block_m(k, p, r, rows, low=True, high=True):
        here = slice(PAD + r, PAD + r + rows)
        mine = slice(r, r + rows)
        centre = fv[k, p, here, :]
        total = weight[0, p, mine, :] * centre
        if low:
            total = total + weight[1, p, mine, :] * fv[k, p - 1, here, :]
        if high:
            total = total + weight[2, p, mine, :] * fv[k, p + 1, here, :]
        total = total + weight[3, p, mine, :] * fv[k, p, PAD + r - 1 : PAD + r - 1 + rows, :]
        total = total + weight[4, p, mine, :] * fv[k, p, PAD + r + 1 : PAD + r + 1 + rows, :]
        minus_z, plus_z = along_z(centre)
        total = total + weight[5, p, mine, :] * minus_z
        total = total + weight[6, p, mine, :] * plus_z
        fw[k, p, here, :] = total
        return total

    def block_a(k, p, r, rows, minus_x=None, plus_x=None):
        here = slice(PAD + r, PAD + r + rows)
        mine = slice(r, r + rows)
        centre = fw[k, p, here, :]
        if minus_x is None:
            minus_x = fw[k, p - 1, here, :]
        if plus_x is None:
            plus_x = fw[k, p + 1, here, :]
        total = centre - weight[7, p, mine, :] * minus_x
        total = total - weight[8, p, mine, :] * plus_x
        total = total - weight[9, p, mine, :] * fw[k, p, PAD + r - 1 : PAD + r - 1 + rows, :]
        total = total - weight[10, p, mine, :] * fw[k, p, PAD + r + 1 : PAD + r + 1 + rows, :]
        minus_z, plus_z = along_z(centre)
        total = total - weight[11, p, mine, :] * minus_z
        total = total - weight[12, p, mine, :] * plus_z
        total = growth * (total - shifts[k] * fv[k, p, here, :])
        fv[k + 1, p, here, :] = total
        return total

    def face_m(k, s, t):
        total = block_m(k, face[s], t * TILE, TILE, low=s == 1, high=s == 0)
        xout[k, s, 1, rows_of(t), :] = total

    def face_a(k, s, t):
        rows = rows_of(t)
        here = slice(PAD + t * TILE, PAD + (t + 1) * TILE)
        beyond = xin[k, s, 1, rows, :] + far[s, rows, :] * fv[k, face[s], here, :]
        if s == 0:
            total = block_a(k, 0, t * TILE, TILE, minus_x=beyond)
        else:
            total = block_a(k, nx - 1, t * TILE, TILE, plus_x=beyond)
        xout[k + 1, s, 0, rows, :] = total

    def start_corners(k):
        for sy in range(2):

            @pl.when(there[sy])
            def _():
                for sx in range(2):
                    corner_copy(k, sx, sy).start()

    def send_corners(k):
        for sy in range(2):
            for sx in range(2):
                row = PAD + edge[sy]
                cout[4 * k + 2 * sx + sy, :, :] = fv[k, face[sx], row : row + 1, :]
        start_corners(k)

    def send_y(k):
        for s in range(2):
            row = PAD + edge[s]

            @pl.when(there[s])
            def _():
                for p in range(nx):
                    yout[k, s, 0, p : p + 1, :] = fv[k, p, row : row + 1, :]
                    yout[k, s, 1, p : p + 1, :] = fw[k, p, row : row + 1, :]
                y_copy(k, s).start()

    def finish_edges(k):
        for sy in range(2):

            @pl.when(there[sy])
            def _():
                for sx in range(2):
                    corner_copy(k, 1 - sx, 1 - sy).wait_recv()
                y_copy(k, 1 - sy).wait_recv()
                row = PAD + edge[sy]
                halo = PAD - 1 if sy == 0 else PAD + ny
                yin[k, sy, 1, :, :] = yin[k, sy, 1, :, :] + near_row[sy] * yout[k, sy, 0, :, :]
                yin[k, sy, 0, :, :] = own_row[sy] * yin[k, sy, 0, :, :]
                for sx in range(2):
                    p, q = face[sx], edge[sy]
                    line = cin[4 * k + 2 * sx + sy, :, :]
                    yin[k, sy, 1, p : p + 1, :] = yin[k, sy, 1, p : p + 1, :] + near_corner[sy, sx : sx + 1, :] * line
                    xin[k, sx, 1, q : q + 1, :] = xin[k, sx, 1, q : q + 1, :] + far_edge[sx, sy : sy + 1, :] * line
                for p in range(nx):
                    fw[k, p, halo : halo + 1, :] = yin[k, sy, 1, p : p + 1, :]
                    fw[k, p, row : row + 1, :] = fw[k, p, row : row + 1, :] + yin[k, sy, 0, p : p + 1, :]

    def products(i, planes, start, size):
        def add(p, totals):
            a = fv[i, p, pl.ds(PAD + start, size), :]
            return tuple(
                total + jnp.sum((a * fv[j, p, pl.ds(PAD + start, size), :]).reshape(size // 8, 8, nz), axis=0)
                for j, total in enumerate(totals)
            )

        totals = lax.fori_loop(*planes, add, tuple(sums[j] for j in range(i + 1)))
        for j, total in enumerate(totals):
            sums[j, :, :] = total

    def forget(i):
        for j in range(i + 1):
            sums[j, :, :] = jnp.zeros((8, nz), jnp.float32)

    def keep(i):
        for j in range(i + 1):
            row = jnp.sum(sums[j], axis=0, keepdims=True)
            flat = row[:, :ROWS]
            for q in range(1, nz // ROWS):
                flat = flat + row[:, q * ROWS : (q + 1) * ROWS]
            n = i * (i + 1) // 2 + j
            part[n : n + 1, :] = flat

    def inner_rows():
        return [(r, min(16, ny - TILE - r)) for r in range(TILE, ny - TILE, 16)]

    def inner_m(k):
        def one(p, c):
            for r, rows in inner_rows():
                block_m(k, p, r, rows)
            return c

        lax.fori_loop(1, nx - 1, one, 0)

    def inner_a(k):
        def one(p, c):
            for r, rows in inner_rows():
                block_a(k, p, r, rows)
            return c

        lax.fori_loop(2, nx - 2, one, 0)

    def edge_m(k):
        def one(p, c):
            block_m(k, p, 0, TILE)
            block_m(k, p, ny - TILE, TILE)
            return c

        lax.fori_loop(1, nx - 1, one, 0)

    def edge_a(k):
        def one(p, c):
            block_a(k, p, 0, TILE)
            block_a(k, p, ny - TILE, TILE)
            return c

        lax.fori_loop(2, nx - 2, one, 0)

    sequence = middle_out(tiles)

    loads[0].wait()
    for sy in range(2):
        for sx in range(2):
            row = PAD + edge[sy]
            cout[2 * sx + sy, :, :] = fv[0, face[sx], row : row + 1, :]
    pl.semaphore_wait(barrier, greetings)
    for s in range(2):
        first_copy(s).start()
    start_corners(0)
    if strides:
        hello_signal(0)
    loads[1].wait()
    loads[2].wait()
    for t in sequence:
        for s in range(2):
            face_m(0, s, t)
            x_copy(0, s, t).start()
            far_copy(s, t).start()
    loads[3].wait()
    for s in range(2):
        r = edge[s]
        for sy in range(2):
            far_corner[s, sy : sy + 1, :] = weight[3 + sy, face[s], edge[sy] : edge[sy] + 1, :]
        far_edge_copy(s).start()
        for p in range(nx):
            own_row[s, p : p + 1, :] = weight[3 + s, p, r : r + 1, :]
        for sx in range(2):
            own_corner[s, sx : sx + 1, :] = weight[1 + sx, face[sx], r : r + 1, :]

        @pl.when(there[s])
        def _():
            for copy in near_copies(s):
                copy.start()

    edge_m(0)
    send_y(0)
    inner_m(0)
    loads[4].wait()
    loads[5].wait()

    def step(k, send):
        inner_a(k)
        forget(k)
        products(k, (0, nx), 0, ny)
        keep(k)
        hello_rounds(k)
        if not send:
            forget(k + 1)
            products(k + 1, (2, nx - 2), TILE, ny - 2 * TILE)
        if k == 0:
            for s in range(2):
                first_copy(1 - s).wait_recv()
        arrived, final, drafted = set(), set(), set()

        def needs(u):
            return {q for q in (u - 1, u, u + 1) if 0 <= q < tiles}

        for t in sequence:
            for s in range(2):
                x_copy(k, 1 - s, t).wait_recv()
                if k == 0:
                    far_copy(1 - s, t).wait_recv()

                here = slice(PAD + t * TILE, PAD + (t + 1) * TILE)
                fw[k, face[s], here, :] = (
                    fw[k, face[s], here, :] + weight[1 + s, face[s], rows_of(t), :] * xin[k, s, 0, rows_of(t), :]
                )
            arrived.add(t)
            last = len(arrived) == tiles
            if last:
                if k == 0:
                    for s in range(2):
                        far_edge_copy(1 - s).wait_recv()

                        @pl.when(there[s])
                        def _():
                            for copy in near_copies(1 - s):
                                copy.wait_recv()

                finish_edges(k)
            ready = [
                u for u in sequence
                if u not in final and needs(u) <= arrived and (last or 0 < u < tiles - 1)
            ]
            for u in ready:
                final.add(u)
            extra = sorted(set().union(*[needs(u) for u in ready]) - final) if send and ready else []
            for u in ready + extra:
                for s in range(2):
                    face_a(k, s, u)
            for u in ready:
                block_a(k, 1, u * TILE, TILE)
                block_a(k, nx - 2, u * TILE, TILE)
            if send:
                if last:
                    send_corners(k + 1)
                for u in ready:
                    for s in range(2):
                        face_m(k + 1, s, u)
                        x_copy(k + 1, s, u).start()
        edge_a(k)
        if send:
            edge_m(k + 1)
            send_y(k + 1)
            inner_m(k + 1)

    for k in range(steps):
        step(k, k + 1 < steps)
    products(steps, (2, nx - 2), 0, TILE)
    products(steps, (2, nx - 2), ny - TILE, TILE)
    products(steps, (0, 2), 0, ny)
    products(steps, (nx - 2, nx), 0, ny)
    keep(steps)

    height = part.shape[0]
    row = lax.broadcasted_iota(jnp.int32, (height, ROWS), 0)
    lane = lax.broadcasted_iota(jnp.int32, (height, ROWS), 1)
    column = jnp.sum(part[...], axis=1, keepdims=True)
    packed = jnp.sum(jnp.where(row == lane, jnp.broadcast_to(column, row.shape), 0.0), axis=0, keepdims=True)
    peers[pl.ds(me, 1), :] = packed

    def peer_copy(d):
        return remote(peers.at[pl.ds(me, 1), :], peers.at[pl.ds(me, 1), :], gs.at[d], gr.at[d], peer(d))

    def peer_start(d, c):
        peer_copy(d).start()
        return c

    def peer_arrive(d, c):
        peer_copy(d).wait_recv()
        return c

    def peer_sent(d, c):
        peer_copy(d).wait_send()
        return c

    lax.fori_loop(1, count, peer_start, 0)

    for k in range(steps):
        for s in range(2):
            for t in range(tiles):
                x_copy(k, s, t).wait_send()

            @pl.when(there[s])
            def _():
                y_copy(k, s).wait_send()
                for sx in range(2):
                    corner_copy(k, sx, s).wait_send()

    for s in range(2):
        first_copy(s).wait_send()
        for t in range(tiles):
            far_copy(s, t).wait_send()
        far_edge_copy(s).wait_send()

        @pl.when(there[s])
        def _():
            for copy in near_copies(s):
                copy.wait_send()

    lax.fori_loop(1, count, peer_arrive, 0)
    total = jnp.sum(peers[...], axis=0, keepdims=True)
    spread = jnp.sum(jnp.where(row == lane, jnp.broadcast_to(total, row.shape), 0.0), axis=1, keepdims=True)
    gram[0:height, :] = jnp.broadcast_to(spread, row.shape)
    for k in range(steps):
        gram[height + k : height + k + 1, :] = jnp.full((1, ROWS), shifts[k], jnp.float32)
    lax.fori_loop(1, count, peer_sent, 0)


def small_algebra(gram, steps, cells):
    order = steps + 1
    height = -(-(order * (order + 1) // 2) // 8) * 8
    shifts = [gram[height + k : height + k + 1, :] for k in range(steps)]
    sums = gram[:height] / cells

    def entry(i, j):
        n = max(i, j) * (max(i, j) + 1) // 2 + min(i, j)
        return sums[n : n + 1, :]

    factor = {}
    for i in range(order):
        value = entry(i, i)
        for k in range(i):
            value = value - factor[k, i] * factor[k, i]
        factor[i, i] = jnp.sqrt(value)
        for j in range(i + 1, order):
            value = entry(i, j)
            for k in range(i):
                value = value - factor[k, i] * factor[k, j]
            factor[i, j] = value / factor[i, i]
    inverse = {}
    for j in range(order):
        inverse[j, j] = 1.0 / factor[j, j]
        for i in range(j - 1, -1, -1):
            value = factor[i, i + 1] * inverse[i + 1, j]
            for k in range(i + 2, j + 1):
                value = value + factor[i, k] * inverse[k, j]
            inverse[i, j] = -value / factor[i, i]
    zero = jnp.zeros_like(factor[0, 0])

    def upper(i, j):
        return factor.get((i, j), zero)

    hess = [[upper(i, k) * shifts[k] + upper(i, k + 1) * (1.0 / growth) for k in range(steps)] for i in range(order)]
    target = [upper(i, 0) for i in range(order)]
    for k in range(steps):
        top, below = hess[k][k], hess[k + 1][k]
        radius = jnp.sqrt(top * top + below * below)
        cosine, sine = top / radius, below / radius
        for c in range(k, steps):
            a, b = hess[k][c], hess[k + 1][c]
            hess[k][c] = cosine * a + sine * b
            hess[k + 1][c] = cosine * b - sine * a
        a, b = target[k], target[k + 1]
        target[k] = cosine * a + sine * b
        target[k + 1] = cosine * b - sine * a
    weights = [None] * steps
    for i in range(steps - 1, -1, -1):
        value = target[i]
        for k in range(i + 1, steps):
            value = value - hess[i][k] * weights[k]
        weights[i] = value / hess[i][i]
    combine = []
    for j in range(order):
        value = zero + (1.0 if j == 0 else 0.0)
        if j < steps:
            value = value - shifts[j] * weights[j]
        if j > 0:
            value = value - (1.0 / growth) * weights[j - 1]
        combine.append(value)
    return factor, inverse, weights, combine


def combine_kernel(cells, gram, v, w, basis, factor_out, solution_out, residual, table, basis_v, sol_v, res_v, sem):
    order, nx, ny, nz = basis_v.shape
    steps = order - 1
    pairs = [(j, k) for k in range(order) for j in range(k + 1)]
    tail = len(pairs)

    factor, inverse, weights, combine = small_algebra(gram[...], steps, cells)
    values = [inverse[p] for p in pairs] + weights + combine
    for n, value in enumerate(values):
        table[n] = jnp.broadcast_to(value, table.shape[1:])
    row = lax.broadcasted_iota(jnp.int32, (8, ROWS), 0)
    column = lax.broadcasted_iota(jnp.int32, (8, ROWS), 1)
    whole = jnp.zeros((8, ROWS), jnp.float32)
    for (i, j), value in factor.items():
        whole = jnp.where((row == i) & (column == j), value, whole)
    factor_out[...] = whole[:order, :order]

    def mul(n, x):
        return table[n][None] * x

    deep = 16 if ny % 16 == 0 else 8

    def tile(p, t):
        rows = pl.ds(pl.multiple_of(t * deep, deep), deep)
        for q in range(0, nz, ROWS):
            lanes = slice(q, q + ROWS)
            load = lambda x: x.reshape(deep // 8, 8, ROWS)
            padded = pl.ds(pl.multiple_of(PAD + t * deep, 8), deep)
            fields = [load(v[k, p, padded, lanes]) for k in range(order)]
            for k in range(order):
                total = None
                for j in range(k + 1):
                    term = mul(pairs.index((j, k)), fields[j])
                    total = term if total is None else total + term
                basis_v[k, p, rows, lanes] = total.reshape(deep, ROWS)
            total = mul(tail, load(w[0, p, padded, lanes]))
            for k in range(1, steps):
                total = total + mul(tail + k, load(w[k, p, padded, lanes]))
            sol_v[p, rows, lanes] = total.reshape(deep, ROWS)
            total = mul(tail + steps, fields[0])
            for j in range(1, order):
                total = total + mul(tail + steps + j, fields[j])
            res_v[p, rows, lanes] = total.reshape(deep, ROWS)

    def copies(p):
        return (
            pltpu.make_async_copy(basis_v.at[:, p], basis.at[:, p], sem.at[p, 0]),
            pltpu.make_async_copy(sol_v.at[p], solution_out.at[p], sem.at[p, 1]),
            pltpu.make_async_copy(res_v.at[p], residual.at[p], sem.at[p, 2]),
        )

    def plane(p, c):
        def inner(t, d):
            tile(p, t)
            return d

        lax.fori_loop(0, ny // deep, inner, 0)
        for copy in copies(p):
            copy.start()
        return c

    def finish(p, c):
        for copy in copies(p):
            copy.wait()
        return c

    lax.fori_loop(0, nx, plane, 0)
    lax.fori_loop(0, nx, finish, 0)


def device_body(n_gx, n_gy, rhs, coefs, shifts):
    steps = shifts.shape[0]
    order = steps + 1
    nx, ny, nz = rhs.shape
    f32 = jnp.float32
    grown = (nx, ny + 2 * PAD, nz)
    height = -(-(order * (order + 1) // 2) // 8) * 8
    gram_rows = height + -(-steps // 8) * 8
    tiles = ny // TILE
    hbm = pl.BlockSpec(memory_space=pltpu.HBM)
    vmem = pl.BlockSpec(memory_space=pltpu.VMEM)
    dma = pltpu.SemaphoreType.DMA
    rhs = pltpu.with_memory_space_constraint(rhs, pltpu.HBM)
    coefs = pltpu.with_memory_space_constraint(coefs, pltpu.HBM)
    shifts = pltpu.with_memory_space_constraint(shifts, pltpu.HBM)
    v, w, gram = pl.pallas_call(
        functools.partial(basis_kernel, n_gx, n_gy),
        out_shape=(
            jax.ShapeDtypeStruct((order,) + grown, f32),
            jax.ShapeDtypeStruct((steps,) + grown, f32),
            jax.ShapeDtypeStruct((gram_rows, ROWS), f32),
        ),
        in_specs=[hbm, hbm, hbm],
        out_specs=(vmem, vmem, vmem),
        scratch_shapes=[
            pltpu.VMEM(coefs.shape, f32),
            pltpu.VMEM((height, ROWS), f32),
            pltpu.VMEM((order, 8, nz), f32),
            pltpu.VMEM((n_gx * n_gy, ROWS), f32),
            pltpu.SMEM(shifts.shape, f32),
            pltpu.VMEM((order, 2, 2, ny, nz), f32),
            pltpu.VMEM((steps, 2, 2, ny, nz), f32),
            pltpu.VMEM((order, 2, 2, nx, nz), f32),
            pltpu.VMEM((steps, 2, 2, nx, nz), f32),
            pltpu.VMEM((4 * order, 1, nz), f32),
            pltpu.VMEM((4 * steps, 1, nz), f32),
            pltpu.VMEM((2, ny, nz), f32),
            pltpu.VMEM((2, 2, nz), f32),
            pltpu.VMEM((2, nx, nz), f32),
            pltpu.VMEM((2, 2, nz), f32),
            pltpu.VMEM((2, nx, nz), f32),
            pltpu.VMEM((2, 2, nz), f32),
            pltpu.VMEM((2, 2, nz), f32),
            dma((6,)),
            pltpu.SemaphoreType.REGULAR((16,)),
            dma((2 * steps * tiles,)),
            dma((2 * steps * tiles,)),
            dma((2 * steps,)),
            dma((2 * steps,)),
            dma((4 * steps,)),
            dma((4 * steps,)),
            dma((2, tiles + 4)),
            dma((2, tiles + 4)),
            dma((n_gx * n_gy,)),
            dma((n_gx * n_gy,)),
        ],
        compiler_params=pltpu.CompilerParams(
            collective_id=0, has_side_effects=True, vmem_limit_bytes=32 * 2**20
        ),
        name="basis",
    )(shifts, rhs, coefs)

    cells = float(nx * ny * nz * n_gx * n_gy)
    return pl.pallas_call(
        functools.partial(combine_kernel, cells),
        out_shape=(
            jax.ShapeDtypeStruct((order, nx, ny, nz), f32),
            jax.ShapeDtypeStruct((order, order), f32),
            jax.ShapeDtypeStruct((nx, ny, nz), f32),
            jax.ShapeDtypeStruct((nx, ny, nz), f32),
        ),
        in_specs=[vmem, vmem, vmem],
        out_specs=(hbm, vmem, hbm, hbm),
        scratch_shapes=[
            pltpu.VMEM((order * (order + 1) // 2 + steps + order, 8, ROWS), f32),
            pltpu.VMEM((order, nx, ny, nz), f32),
            pltpu.VMEM((nx, ny, nz), f32),
            pltpu.VMEM((nx, ny, nz), f32),
            dma((nx, 3)),
        ],
        compiler_params=pltpu.CompilerParams(vmem_limit_bytes=32 * 2**20),
        name="combine",
    )(gram, v, w)


def solution(mesh):
    placed = (P("gx", "gy", None), P(None, "gx", "gy", None), P())
    return jax.shard_map(
        functools.partial(device_body, mesh.shape["gx"], mesh.shape["gy"]),
        mesh=mesh,
        in_specs=placed,
        out_specs=(P(None, "gx", "gy", None), P(), P("gx", "gy", None), P("gx", "gy", None)),
        check_vma=False,
    )
```

```python
import functools

import jax
import jax.numpy as jnp
from jax import lax
from jax.experimental import pallas as pl
from jax.experimental.pallas import tpu as pltpu
from jax.sharding import PartitionSpec as P

growth = 2.0
MESH = pl.DeviceIdType.MESH
PAD = 8
ROWS = 128
TILE = 8


def middle_out(count):
    low, high = (count - 1) // 2, (count - 1) // 2 + 1
    order = []
    while low >= 0 or high < count:
        if high < count:
            order.append(high)
            high += 1
        if low >= 0:
            order.append(low)
            low -= 1
    return order


def basis_kernel(
    n_gx, n_gy, shifts_hbm, rhs, coefs, fv, fw, gram,
    weight, part, sums, peers, shifts, xout, xin, yout, yin, cout, cin,
    far, far_corner, own_row, own_corner, near_row, near_corner, far_edge,
    load_sem, hello, xs, xr, ys, yr, cs, cr, fs, fr, gs, gr,
):
    steps = shifts.shape[0]
    order = steps + 1
    nx, ny, nz = rhs.shape
    tiles = ny // TILE
    assert tiles >= 4 and nx >= 4 and ny % TILE == 0
    body = slice(PAD, PAD + ny)
    face = (0, nx - 1)
    edge = (0, ny - 1)
    gx, gy = lax.axis_index("gx"), lax.axis_index("gy")
    beside_x = (lax.rem(gx + n_gx - 1, n_gx), lax.rem(gx + 1, n_gx))
    beside_y = (jnp.maximum(gy - 1, 0), jnp.minimum(gy + 1, n_gy - 1))
    there = (gy > 0, gy < n_gy - 1)
    count = n_gx * n_gy
    me = gx * n_gy + gy

    loads = [
        pltpu.make_async_copy(rhs, fv.at[0, :, body, :], load_sem.at[0]),
        pltpu.make_async_copy(coefs.at[0:7, 0], weight.at[0:7, 0], load_sem.at[1]),
        pltpu.make_async_copy(coefs.at[0:7, nx - 1], weight.at[0:7, nx - 1], load_sem.at[2]),
        pltpu.make_async_copy(coefs.at[0:7, 1 : nx - 1], weight.at[0:7, 1 : nx - 1], load_sem.at[3]),
        pltpu.make_async_copy(coefs.at[7:13], weight.at[7:13], load_sem.at[4]),
        pltpu.make_async_copy(shifts_hbm, shifts, load_sem.at[5]),
    ]
    cin[...] = jnp.zeros_like(cin)

    barrier = pltpu.get_barrier_semaphore()

    def peer(d):
        other = lax.rem(me + d, count)
        return {"gx": lax.div(other, n_gy), "gy": lax.rem(other, n_gy)}

    def greet(device):
        pl.semaphore_signal(barrier, inc=1, device_id=device, device_id_type=MESH)

    for x in beside_x:
        greet({"gx": x})
    for s in range(2):

        @pl.when(there[s])
        def _():
            greet({"gy": beside_y[s]})
            for x in beside_x:
                greet({"gx": x, "gy": beside_y[s]})

    greet(peer(1))
    greet(peer(count - 1))
    for load in loads:
        load.start()
    greetings = 4 + 3 * (there[0].astype(jnp.int32) + there[1].astype(jnp.int32))

    strides = []
    while (2 ** len(strides)) * 2 < count:
        strides.append(2 ** len(strides))

    def hello_signal(r):
        for d in (strides[r], count - strides[r]):
            pl.semaphore_signal(hello.at[r], inc=1, device_id=peer(d), device_id_type=MESH)

    def hello_rounds(k):
        share = -(-len(strides) // steps)
        for r in range(k * share, min((k + 1) * share, len(strides))):
            pl.semaphore_wait(hello.at[r], 2)
            if r + 1 < len(strides):
                hello_signal(r + 1)

    part[...] = jnp.zeros_like(part)
    blank = jnp.zeros((PAD, nz), jnp.float32)
    for fields in (fv, fw):

        def clear(p, c):
            for k in range(fields.shape[0]):
                fields[k, p, 0:PAD, :] = blank
                fields[k, p, PAD + ny : PAD + ny + PAD, :] = blank
            return c

        lax.fori_loop(0, nx, clear, 0)

    def rows_of(t):
        return slice(t * TILE, (t + 1) * TILE)

    def remote(source, target, send, receive, device):
        return pltpu.make_async_remote_copy(
            src_ref=source, dst_ref=target, send_sem=send, recv_sem=receive,
            device_id=device, device_id_type=MESH,
        )

    def x_copy(k, s, t):
        n, m = (2 * k + s) * tiles + t, (2 * k + 1 - s) * tiles + t
        kinds = slice(1 if k == 0 else 0, 2)
        return remote(
            xout.at[k, s, kinds, rows_of(t), :], xin.at[k, 1 - s, kinds, rows_of(t), :],
            xs.at[n], xr.at[m], {"gx": beside_x[s]},
        )

    def y_copy(k, s):
        kinds = slice(1 if k == 0 else 0, 2)
        return remote(
            yout.at[k, s, kinds], yin.at[k, 1 - s, kinds],
            ys.at[2 * k + s], yr.at[2 * k + 1 - s], {"gy": beside_y[s]},
        )

    def first_y_copy(s):
        n, m = 2 * steps + s, 2 * steps + 1 - s
        return remote(yout.at[0, s, 0], yin.at[0, 1 - s, 0], ys.at[n], yr.at[m], {"gy": beside_y[s]})

    def corner_copy(k, sx, sy):
        n, m = 4 * k + 2 * sx + sy, 4 * k + 2 * (1 - sx) + 1 - sy
        return remote(
            cout.at[n], cin.at[m], cs.at[n], cr.at[m], {"gx": beside_x[sx], "gy": beside_y[sy]}
        )

    def first_copy(s, t):
        n = tiles + 3 + t
        return remote(
            rhs.at[face[s], rows_of(t), :], xin.at[0, 1 - s, 0, rows_of(t), :],
            fs.at[s, n], fr.at[1 - s, n], {"gx": beside_x[s]},
        )

    def far_copy(s, t):
        return remote(
            coefs.at[1 + s, face[s], rows_of(t), :], far.at[1 - s, rows_of(t), :],
            fs.at[s, t], fr.at[1 - s, t], {"gx": beside_x[s]},
        )

    def far_edge_copy(s):
        return remote(
            far_corner.at[s], far_edge.at[1 - s], fs.at[s, tiles], fr.at[1 - s, tiles], {"gx": beside_x[s]}
        )

    def near_copies(s):
        device = {"gy": beside_y[s]}
        return (
            remote(own_row.at[s], near_row.at[1 - s], fs.at[s, tiles + 1], fr.at[1 - s, tiles + 1], device),
            remote(own_corner.at[s], near_corner.at[1 - s], fs.at[s, tiles + 2], fr.at[1 - s, tiles + 2], device),
        )

    def along_z(centre):
        lane = lax.broadcasted_iota(jnp.int32, centre.shape, 1)
        return (
            jnp.where(lane == 0, 0.0, pltpu.roll(centre, 1, 1)),
            jnp.where(lane == nz - 1, 0.0, pltpu.roll(centre, nz - 1, 1)),
        )

    def block_m(k, p, r, rows, low=True, high=True):
        here = slice(PAD + r, PAD + r + rows)
        mine = slice(r, r + rows)
        centre = fv[k, p, here, :]
        total = weight[0, p, mine, :] * centre
        if low:
            total = total + weight[1, p, mine, :] * fv[k, p - 1, here, :]
        if high:
            total = total + weight[2, p, mine, :] * fv[k, p + 1, here, :]
        total = total + weight[3, p, mine, :] * fv[k, p, PAD + r - 1 : PAD + r - 1 + rows, :]
        total = total + weight[4, p, mine, :] * fv[k, p, PAD + r + 1 : PAD + r + 1 + rows, :]
        minus_z, plus_z = along_z(centre)
        total = total + weight[5, p, mine, :] * minus_z
        total = total + weight[6, p, mine, :] * plus_z
        fw[k, p, here, :] = total
        return total

    def block_a(k, p, r, rows, minus_x=None, plus_x=None):
        here = slice(PAD + r, PAD + r + rows)
        mine = slice(r, r + rows)
        centre = fw[k, p, here, :]
        if minus_x is None:
            minus_x = fw[k, p - 1, here, :]
        if plus_x is None:
            plus_x = fw[k, p + 1, here, :]
        total = centre - weight[7, p, mine, :] * minus_x
        total = total - weight[8, p, mine, :] * plus_x
        total = total - weight[9, p, mine, :] * fw[k, p, PAD + r - 1 : PAD + r - 1 + rows, :]
        total = total - weight[10, p, mine, :] * fw[k, p, PAD + r + 1 : PAD + r + 1 + rows, :]
        minus_z, plus_z = along_z(centre)
        total = total - weight[11, p, mine, :] * minus_z
        total = total - weight[12, p, mine, :] * plus_z
        total = growth * (total - shifts[k] * fv[k, p, here, :])
        fv[k + 1, p, here, :] = total
        return total

    def face_m(k, s, t):
        total = block_m(k, face[s], t * TILE, TILE, low=s == 1, high=s == 0)
        xout[k, s, 1, rows_of(t), :] = total

    def face_a(k, s, t):
        rows = rows_of(t)
        here = slice(PAD + t * TILE, PAD + (t + 1) * TILE)
        beyond = xin[k, s, 1, rows, :]
        if k > 0:
            beyond = beyond + far[s, rows, :] * fv[k, face[s], here, :]
        if s == 0:
            total = block_a(k, 0, t * TILE, TILE, minus_x=beyond)
        else:
            total = block_a(k, nx - 1, t * TILE, TILE, plus_x=beyond)
        xout[k + 1, s, 0, rows, :] = total

    def stage_corners(k, sy):
        row = PAD + edge[sy]
        for sx in range(2):
            cout[4 * k + 2 * sx + sy, :, :] = fv[k, face[sx], row : row + 1, :]

    def start_corners(k, sy):
        @pl.when(there[sy])
        def _():
            for sx in range(2):
                corner_copy(k, sx, sy).start()

    def stage_y(k, s, kind, fields):
        row = PAD + edge[s]
        for p in range(nx):
            yout[k, s, kind, p : p + 1, :] = fields[k, p, row : row + 1, :]

    def send_y(k, s):
        @pl.when(there[s])
        def _():
            if k > 0:
                stage_y(k, s, 0, fv)
            stage_y(k, s, 1, fw)
            y_copy(k, s).start()

    def own_edge(k, sy):
        row = PAD + edge[sy]
        yin[k, sy, 0, :, :] = own_row[sy] * yin[k, sy, 0, :, :]
        for p in range(nx):
            fw[k, p, row : row + 1, :] = fw[k, p, row : row + 1, :] + yin[k, sy, 0, p : p + 1, :]

    def finish_edge(k, sy):
        @pl.when(there[sy])
        def _():
            for sx in range(2):
                corner_copy(k, 1 - sx, 1 - sy).wait_recv()
            y_copy(k, 1 - sy).wait_recv()
            halo = PAD - 1 if sy == 0 else PAD + ny
            yin[k, sy, 1, :, :] = yin[k, sy, 1, :, :] + near_row[sy] * yout[k, sy, 0, :, :]
            for sx in range(2):
                p, q = face[sx], edge[sy]
                line = cin[4 * k + 2 * sx + sy, :, :]
                yin[k, sy, 1, p : p + 1, :] = yin[k, sy, 1, p : p + 1, :] + near_corner[sy, sx : sx + 1, :] * line
                if k > 0:
                    xin[k, sx, 1, q : q + 1, :] = xin[k, sx, 1, q : q + 1, :] + far_edge[sx, sy : sy + 1, :] * line
            if k > 0:
                own_edge(k, sy)
            for p in range(nx):
                fw[k, p, halo : halo + 1, :] = yin[k, sy, 1, p : p + 1, :]

    def products(i, planes, start, size):
        def add(p, totals):
            a = fv[i, p, pl.ds(PAD + start, size), :]
            return tuple(
                total + jnp.sum((a * fv[j, p, pl.ds(PAD + start, size), :]).reshape(size // 8, 8, nz), axis=0)
                for j, total in enumerate(totals)
            )

        totals = lax.fori_loop(*planes, add, tuple(sums[j] for j in range(i + 1)))
        for j, total in enumerate(totals):
            sums[j, :, :] = total

    def forget(i):
        for j in range(i + 1):
            sums[j, :, :] = jnp.zeros((8, nz), jnp.float32)

    def keep(i):
        for j in range(i + 1):
            row = jnp.sum(sums[j], axis=0, keepdims=True)
            flat = row[:, :ROWS]
            for q in range(1, nz // ROWS):
                flat = flat + row[:, q * ROWS : (q + 1) * ROWS]
            n = i * (i + 1) // 2 + j
            part[n : n + 1, :] = flat

    def inner_rows():
        return [(r, min(16, ny - TILE - r)) for r in range(TILE, ny - TILE, 16)]

    def inner_m(k):
        def one(p, c):
            for r, rows in inner_rows():
                block_m(k, p, r, rows)
            return c

        lax.fori_loop(1, nx - 1, one, 0)

    def inner_a(k):
        def one(p, c):
            for r, rows in inner_rows():
                block_a(k, p, r, rows)
            return c

        lax.fori_loop(2, nx - 2, one, 0)

    def edge_m(k, sy):
        def one(p, c):
            block_m(k, p, (0, ny - TILE)[sy], TILE)
            return c

        lax.fori_loop(1, nx - 1, one, 0)

    def edge_a(k, sy):
        def one(p, c):
            block_a(k, p, (0, ny - TILE)[sy], TILE)
            return c

        lax.fori_loop(2, nx - 2, one, 0)

    sequence = middle_out(tiles)

    middle = sequence[: tiles // 2]
    outside = sequence[tiles // 2 :]

    loads[0].wait()
    for sy in range(2):
        stage_corners(0, sy)
        stage_y(0, sy, 0, fv)
    pl.semaphore_wait(barrier, greetings)
    for t in sequence:
        for s in range(2):
            first_copy(s, t).start()
    for s in range(2):
        start_corners(0, s)

        @pl.when(there[s])
        def _():
            first_y_copy(s).start()

    if strides:
        hello_signal(0)
    for t in middle:
        for s in range(2):
            far_copy(s, t).start()
    for load in loads[1:4]:
        load.wait()
    for s in range(2):
        r = edge[s]
        for sy in range(2):
            far_corner[s, sy : sy + 1, :] = weight[3 + sy, face[s], edge[sy] : edge[sy] + 1, :]
        for p in range(nx):
            own_row[s, p : p + 1, :] = weight[3 + s, p, r : r + 1, :]
        for sx in range(2):
            own_corner[s, sx : sx + 1, :] = weight[1 + sx, face[sx], r : r + 1, :]

        @pl.when(there[s])
        def _():
            for copy in near_copies(s):
                copy.start()

    for t in sequence:
        for s in range(2):
            face_m(0, s, t)
    for sy in range(2):
        edge_m(0, sy)
        send_y(0, sy)
    for t in sequence:
        for sy in range(2):
            if t == (0, tiles - 1)[sy]:

                @pl.when(there[sy])
                def _():
                    first_y_copy(1 - sy).wait_recv()
                    own_edge(0, sy)

        here = slice(PAD + t * TILE, PAD + (t + 1) * TILE)
        for s in range(2):
            first_copy(1 - s, t).wait_recv()
            total = fw[0, face[s], here, :] + weight[1 + s, face[s], rows_of(t), :] * xin[0, s, 0, rows_of(t), :]
            fw[0, face[s], here, :] = total
            xout[0, s, 1, rows_of(t), :] = total
            x_copy(0, s, t).start()
    for t in outside:
        for s in range(2):
            far_copy(s, t).start()
    for s in range(2):
        far_edge_copy(s).start()
    inner_m(0)
    loads[4].wait()
    loads[5].wait()

    def step(k, send):
        inner_a(k)
        forget(k)
        products(k, (0, nx), 0, ny)
        keep(k)
        hello_rounds(k)
        if not send:
            forget(k + 1)
            products(k + 1, (2, nx - 2), TILE, ny - 2 * TILE)
        arrived, final = set(), set()

        def needs(u):
            return {q for q in (u - 1, u, u + 1) if 0 <= q < tiles}

        for t in sequence:
            sides = [sy for sy in range(2) if t == (0, tiles - 1)[sy]]
            here = slice(PAD + t * TILE, PAD + (t + 1) * TILE)
            for s in range(2):
                x_copy(k, 1 - s, t).wait_recv()
                if k == 1:
                    far_copy(1 - s, t).wait_recv()
                if k > 0:
                    fw[k, face[s], here, :] = (
                        fw[k, face[s], here, :]
                        + weight[1 + s, face[s], rows_of(t), :] * xin[k, s, 0, rows_of(t), :]
                    )
            arrived.add(t)
            for sy in sides:
                if k == 1 and sy == (1 if tiles > 1 else 0):
                    for s in range(2):
                        far_edge_copy(1 - s).wait_recv()
                if k == 0:

                    @pl.when(there[sy])
                    def _():
                        for copy in near_copies(1 - sy):
                            copy.wait_recv()

                finish_edge(k, sy)
            ready = [u for u in sequence if u not in final and needs(u) <= arrived]
            for u in ready:
                final.add(u)
            extra = sorted(set().union(*[needs(u) for u in ready]) - final) if send and ready else []
            for u in ready + extra:
                for s in range(2):
                    face_a(k, s, u)
            for u in ready:
                block_a(k, 1, u * TILE, TILE)
                block_a(k, nx - 2, u * TILE, TILE)
            if send:
                for sy in sides:
                    stage_corners(k + 1, sy)
                    start_corners(k + 1, sy)
                for u in ready:
                    for s in range(2):
                        face_m(k + 1, s, u)
                        x_copy(k + 1, s, u).start()
            for sy in sides:
                edge_a(k, sy)
                if send:
                    edge_m(k + 1, sy)
                    send_y(k + 1, sy)
                else:
                    products(k + 1, (2, nx - 2), (0, ny - TILE)[sy], TILE)
        if send:
            inner_m(k + 1)

    for k in range(steps):
        step(k, k + 1 < steps)
    products(steps, (0, 2), 0, ny)
    products(steps, (nx - 2, nx), 0, ny)
    keep(steps)

    height = part.shape[0]
    row = lax.broadcasted_iota(jnp.int32, (height, ROWS), 0)
    lane = lax.broadcasted_iota(jnp.int32, (height, ROWS), 1)
    column = jnp.sum(part[...], axis=1, keepdims=True)
    packed = jnp.sum(jnp.where(row == lane, jnp.broadcast_to(column, row.shape), 0.0), axis=0, keepdims=True)
    peers[pl.ds(me, 1), :] = packed

    def peer_copy(d):
        return remote(peers.at[pl.ds(me, 1), :], peers.at[pl.ds(me, 1), :], gs.at[d], gr.at[d], peer(d))

    def peer_start(d, c):
        peer_copy(d).start()
        return c

    def peer_arrive(d, c):
        peer_copy(d).wait_recv()
        return c

    def peer_sent(d, c):
        peer_copy(d).wait_send()
        return c

    lax.fori_loop(1, count, peer_start, 0)

    for k in range(steps):
        for s in range(2):
            for t in range(tiles):
                x_copy(k, s, t).wait_send()

            @pl.when(there[s])
            def _():
                y_copy(k, s).wait_send()
                for sx in range(2):
                    corner_copy(k, sx, s).wait_send()

    for s in range(2):
        for t in range(tiles):
            first_copy(s, t).wait_send()
            far_copy(s, t).wait_send()
        far_edge_copy(s).wait_send()

        @pl.when(there[s])
        def _():
            first_y_copy(s).wait_send()
            for copy in near_copies(s):
                copy.wait_send()

    lax.fori_loop(1, count, peer_arrive, 0)
    total = jnp.sum(peers[...], axis=0, keepdims=True)
    spread = jnp.sum(jnp.where(row == lane, jnp.broadcast_to(total, row.shape), 0.0), axis=1, keepdims=True)
    gram[0:height, :] = jnp.broadcast_to(spread, row.shape)
    for k in range(steps):
        gram[height + k : height + k + 1, :] = jnp.full((1, ROWS), shifts[k], jnp.float32)
    lax.fori_loop(1, count, peer_sent, 0)


def small_algebra(gram, steps, cells):
    order = steps + 1
    height = -(-(order * (order + 1) // 2) // 8) * 8
    shifts = [gram[height + k : height + k + 1, :] for k in range(steps)]
    sums = gram[:height] / cells

    def entry(i, j):
        n = max(i, j) * (max(i, j) + 1) // 2 + min(i, j)
        return sums[n : n + 1, :]

    factor = {}
    for i in range(order):
        value = entry(i, i)
        for k in range(i):
            value = value - factor[k, i] * factor[k, i]
        factor[i, i] = jnp.sqrt(value)
        for j in range(i + 1, order):
            value = entry(i, j)
            for k in range(i):
                value = value - factor[k, i] * factor[k, j]
            factor[i, j] = value / factor[i, i]
    inverse = {}
    for j in range(order):
        inverse[j, j] = 1.0 / factor[j, j]
        for i in range(j - 1, -1, -1):
            value = factor[i, i + 1] * inverse[i + 1, j]
            for k in range(i + 2, j + 1):
                value = value + factor[i, k] * inverse[k, j]
            inverse[i, j] = -value / factor[i, i]
    zero = jnp.zeros_like(factor[0, 0])

    def upper(i, j):
        return factor.get((i, j), zero)

    hess = [[upper(i, k) * shifts[k] + upper(i, k + 1) * (1.0 / growth) for k in range(steps)] for i in range(order)]
    target = [upper(i, 0) for i in range(order)]
    for k in range(steps):
        top, below = hess[k][k], hess[k + 1][k]
        radius = jnp.sqrt(top * top + below * below)
        cosine, sine = top / radius, below / radius
        for c in range(k, steps):
            a, b = hess[k][c], hess[k + 1][c]
            hess[k][c] = cosine * a + sine * b
            hess[k + 1][c] = cosine * b - sine * a
        a, b = target[k], target[k + 1]
        target[k] = cosine * a + sine * b
        target[k + 1] = cosine * b - sine * a
    weights = [None] * steps
    for i in range(steps - 1, -1, -1):
        value = target[i]
        for k in range(i + 1, steps):
            value = value - hess[i][k] * weights[k]
        weights[i] = value / hess[i][i]
    combine = []
    for j in range(order):
        value = zero + (1.0 if j == 0 else 0.0)
        if j < steps:
            value = value - shifts[j] * weights[j]
        if j > 0:
            value = value - (1.0 / growth) * weights[j - 1]
        combine.append(value)
    return factor, inverse, weights, combine


def combine_kernel(cells, gram, v, w, basis, factor_out, solution_out, residual, table, basis_v, sol_v, res_v, factor_v, sem, factor_sem):
    order, nx, ny, nz = basis_v.shape
    steps = order - 1
    pairs = [(j, k) for k in range(order) for j in range(k + 1)]
    tail = len(pairs)

    factor, inverse, weights, combine = small_algebra(gram[...], steps, cells)
    values = [inverse[p] for p in pairs] + weights + combine
    for n, value in enumerate(values):
        table[n] = jnp.broadcast_to(value, table.shape[1:])
    row = lax.broadcasted_iota(jnp.int32, (8, ROWS), 0)
    column = lax.broadcasted_iota(jnp.int32, (8, ROWS), 1)
    whole = jnp.zeros((8, ROWS), jnp.float32)
    for (i, j), value in factor.items():
        whole = jnp.where((row == i) & (column == j), value, whole)
    factor_v[...] = whole[:order, :order]
    factor_copy = pltpu.make_async_copy(factor_v, factor_out, factor_sem)
    factor_copy.start()

    def mul(n, x):
        return table[n][None] * x

    deep = 16 if ny % 16 == 0 else 8

    def tile(p, t):
        rows = pl.ds(pl.multiple_of(t * deep, deep), deep)
        for q in range(0, nz, ROWS):
            lanes = slice(q, q + ROWS)
            load = lambda x: x.reshape(deep // 8, 8, ROWS)
            padded = pl.ds(pl.multiple_of(PAD + t * deep, 8), deep)
            fields = [load(v[k, p, padded, lanes]) for k in range(order)]
            for k in range(order):
                total = None
                for j in range(k + 1):
                    term = mul(pairs.index((j, k)), fields[j])
                    total = term if total is None else total + term
                basis_v[k, p, rows, lanes] = total.reshape(deep, ROWS)
            total = mul(tail, load(w[0, p, padded, lanes]))
            for k in range(1, steps):
                total = total + mul(tail + k, load(w[k, p, padded, lanes]))
            sol_v[p, rows, lanes] = total.reshape(deep, ROWS)
            total = mul(tail + steps, fields[0])
            for j in range(1, order):
                total = total + mul(tail + steps + j, fields[j])
            res_v[p, rows, lanes] = total.reshape(deep, ROWS)

    def copies(p):
        return (
            pltpu.make_async_copy(basis_v.at[:, p], basis.at[:, p], sem.at[p, 0]),
            pltpu.make_async_copy(sol_v.at[p], solution_out.at[p], sem.at[p, 1]),
            pltpu.make_async_copy(res_v.at[p], residual.at[p], sem.at[p, 2]),
        )

    def plane(p, c):
        def inner(t, d):
            tile(p, t)
            return d

        lax.fori_loop(0, ny // deep, inner, 0)
        for copy in copies(p):
            copy.start()
        return c

    def finish(p, c):
        for copy in copies(p):
            copy.wait()
        return c

    lax.fori_loop(0, nx, plane, 0)
    lax.fori_loop(0, nx, finish, 0)
    factor_copy.wait()


def device_body(n_gx, n_gy, rhs, coefs, shifts):
    steps = shifts.shape[0]
    order = steps + 1
    nx, ny, nz = rhs.shape
    f32 = jnp.float32
    grown = (nx, ny + 2 * PAD, nz)
    height = -(-(order * (order + 1) // 2) // 8) * 8
    gram_rows = height + -(-steps // 8) * 8
    tiles = ny // TILE
    hbm = pl.BlockSpec(memory_space=pltpu.HBM)
    vmem = pl.BlockSpec(memory_space=pltpu.VMEM)
    dma = pltpu.SemaphoreType.DMA
    rhs = pltpu.with_memory_space_constraint(rhs, pltpu.HBM)
    coefs = pltpu.with_memory_space_constraint(coefs, pltpu.HBM)
    shifts = pltpu.with_memory_space_constraint(shifts, pltpu.HBM)
    v, w, gram = pl.pallas_call(
        functools.partial(basis_kernel, n_gx, n_gy),
        out_shape=(
            jax.ShapeDtypeStruct((order,) + grown, f32),
            jax.ShapeDtypeStruct((steps,) + grown, f32),
            jax.ShapeDtypeStruct((gram_rows, ROWS), f32),
        ),
        in_specs=[hbm, hbm, hbm],
        out_specs=(vmem, vmem, vmem),
        scratch_shapes=[
            pltpu.VMEM(coefs.shape, f32),
            pltpu.VMEM((height, ROWS), f32),
            pltpu.VMEM((order, 8, nz), f32),
            pltpu.VMEM((n_gx * n_gy, ROWS), f32),
            pltpu.SMEM(shifts.shape, f32),
            pltpu.VMEM((order, 2, 2, ny, nz), f32),
            pltpu.VMEM((steps, 2, 2, ny, nz), f32),
            pltpu.VMEM((order, 2, 2, nx, nz), f32),
            pltpu.VMEM((steps, 2, 2, nx, nz), f32),
            pltpu.VMEM((4 * order, 1, nz), f32),
            pltpu.VMEM((4 * steps, 1, nz), f32),
            pltpu.VMEM((2, ny, nz), f32),
            pltpu.VMEM((2, 2, nz), f32),
            pltpu.VMEM((2, nx, nz), f32),
            pltpu.VMEM((2, 2, nz), f32),
            pltpu.VMEM((2, nx, nz), f32),
            pltpu.VMEM((2, 2, nz), f32),
            pltpu.VMEM((2, 2, nz), f32),
            dma((6,)),
            pltpu.SemaphoreType.REGULAR((16,)),
            dma((2 * steps * tiles,)),
            dma((2 * steps * tiles,)),
            dma((2 * steps + 2,)),
            dma((2 * steps + 2,)),
            dma((4 * steps,)),
            dma((4 * steps,)),
            dma((2, 2 * tiles + 3)),
            dma((2, 2 * tiles + 3)),
            dma((n_gx * n_gy,)),
            dma((n_gx * n_gy,)),
        ],
        compiler_params=pltpu.CompilerParams(
            collective_id=0, has_side_effects=True, vmem_limit_bytes=32 * 2**20
        ),
        name="basis",
    )(shifts, rhs, coefs)

    cells = float(nx * ny * nz * n_gx * n_gy)
    return pl.pallas_call(
        functools.partial(combine_kernel, cells),
        out_shape=(
            jax.ShapeDtypeStruct((order, nx, ny, nz), f32),
            jax.ShapeDtypeStruct((order, order), f32),
            jax.ShapeDtypeStruct((nx, ny, nz), f32),
            jax.ShapeDtypeStruct((nx, ny, nz), f32),
        ),
        in_specs=[vmem, vmem, vmem],
        out_specs=(hbm, hbm, hbm, hbm),
        scratch_shapes=[
            pltpu.VMEM((order * (order + 1) // 2 + steps + order, 8, ROWS), f32),
            pltpu.VMEM((order, nx, ny, nz), f32),
            pltpu.VMEM((nx, ny, nz), f32),
            pltpu.VMEM((nx, ny, nz), f32),
            pltpu.VMEM((order, order), f32),
            dma((nx, 3)),
            dma,
        ],
        compiler_params=pltpu.CompilerParams(vmem_limit_bytes=32 * 2**20),
        name="combine",
    )(gram, v, w)


def solution(mesh):
    placed = (P("gx", "gy", None), P(None, "gx", "gy", None), P())
    return jax.shard_map(
        functools.partial(device_body, mesh.shape["gx"], mesh.shape["gy"]),
        mesh=mesh,
        in_specs=placed,
        out_specs=(P(None, "gx", "gy", None), P(), P("gx", "gy", None), P("gx", "gy", None)),
        check_vma=False,
    )
```

```python
import functools

import jax
import jax.numpy as jnp
from jax import lax
from jax.experimental import pallas as pl
from jax.experimental.pallas import tpu as pltpu
from jax.sharding import PartitionSpec as P

growth = 2.0
MESH = pl.DeviceIdType.MESH
PAD = 8
ROWS = 128
TILE = 8


def middle_out(count):
    low, high = (count - 1) // 2, (count - 1) // 2 + 1
    order = []
    while low >= 0 or high < count:
        if high < count:
            order.append(high)
            high += 1
        if low >= 0:
            order.append(low)
            low -= 1
    return order


def basis_kernel(
    n_gx, n_gy, shifts_hbm, rhs, coefs, fv, fw, gram,
    weight, part, sums, peers, shifts, xout, xin, yout, yin, cout, cin,
    far, far_corner, own_row, own_corner, near_row, near_corner, far_edge,
    load_sem, hello, xs, xr, ys, yr, cs, cr, fs, fr, gs, gr,
):
    steps = shifts.shape[0]
    order = steps + 1
    nx, ny, nz = rhs.shape
    tiles = ny // TILE
    assert tiles >= 4 and nx >= 4 and ny % TILE == 0
    body = slice(PAD, PAD + ny)
    face = (0, nx - 1)
    edge = (0, ny - 1)
    gx, gy = lax.axis_index("gx"), lax.axis_index("gy")
    beside_x = (lax.rem(gx + n_gx - 1, n_gx), lax.rem(gx + 1, n_gx))
    beside_y = (jnp.maximum(gy - 1, 0), jnp.minimum(gy + 1, n_gy - 1))
    there = (gy > 0, gy < n_gy - 1)
    count = n_gx * n_gy
    me = gx * n_gy + gy

    loads = [
        pltpu.make_async_copy(rhs, fv.at[0, :, body, :], load_sem.at[0]),
        pltpu.make_async_copy(coefs.at[0:7, 0], weight.at[0:7, 0], load_sem.at[1]),
        pltpu.make_async_copy(coefs.at[0:7, nx - 1], weight.at[0:7, nx - 1], load_sem.at[2]),
        pltpu.make_async_copy(coefs.at[0:7, 1 : nx - 1], weight.at[0:7, 1 : nx - 1], load_sem.at[3]),
        pltpu.make_async_copy(coefs.at[7:13], weight.at[7:13], load_sem.at[4]),
        pltpu.make_async_copy(shifts_hbm, shifts, load_sem.at[5]),
    ]
    cin[...] = jnp.zeros_like(cin)

    barrier = pltpu.get_barrier_semaphore()

    def peer(d):
        other = lax.rem(me + d, count)
        return {"gx": lax.div(other, n_gy), "gy": lax.rem(other, n_gy)}

    def greet(device):
        pl.semaphore_signal(barrier, inc=1, device_id=device, device_id_type=MESH)

    for x in beside_x:
        greet({"gx": x})
    for s in range(2):

        @pl.when(there[s])
        def _():
            greet({"gy": beside_y[s]})
            for x in beside_x:
                greet({"gx": x, "gy": beside_y[s]})

    greet(peer(1))
    greet(peer(count - 1))
    for load in loads:
        load.start()
    greetings = 4 + 3 * (there[0].astype(jnp.int32) + there[1].astype(jnp.int32))

    strides = []
    while (2 ** len(strides)) * 2 < count:
        strides.append(2 ** len(strides))

    def hello_signal(r):
        for d in (strides[r], count - strides[r]):
            pl.semaphore_signal(hello.at[r], inc=1, device_id=peer(d), device_id_type=MESH)

    def hello_rounds(k):
        share = -(-len(strides) // steps)
        for r in range(k * share, min((k + 1) * share, len(strides))):
            pl.semaphore_wait(hello.at[r], 2)
            if r + 1 < len(strides):
                hello_signal(r + 1)

    part[...] = jnp.zeros_like(part)
    blank = jnp.zeros((PAD, nz), jnp.float32)
    for fields in (fv, fw):

        def clear(p, c):
            for k in range(fields.shape[0]):
                fields[k, p, 0:PAD, :] = blank
                fields[k, p, PAD + ny : PAD + ny + PAD, :] = blank
            return c

        lax.fori_loop(0, nx, clear, 0)

    def rows_of(t):
        return slice(t * TILE, (t + 1) * TILE)

    def remote(source, target, send, receive, device):
        return pltpu.make_async_remote_copy(
            src_ref=source, dst_ref=target, send_sem=send, recv_sem=receive,
            device_id=device, device_id_type=MESH,
        )

    def x_copy(k, s, t):
        n, m = (2 * k + s) * tiles + t, (2 * k + 1 - s) * tiles + t
        kinds = slice(1 if k == 0 else 0, 2)
        return remote(
            xout.at[k, s, kinds, rows_of(t), :], xin.at[k, 1 - s, kinds, rows_of(t), :],
            xs.at[n], xr.at[m], {"gx": beside_x[s]},
        )

    def y_copy(k, s):
        return remote(
            yout.at[k, s], yin.at[k, 1 - s], ys.at[2 * k + s], yr.at[2 * k + 1 - s], {"gy": beside_y[s]}
        )

    def corner_copy(k, sx, sy):
        n, m = 4 * k + 2 * sx + sy, 4 * k + 2 * (1 - sx) + 1 - sy
        return remote(
            cout.at[n], cin.at[m], cs.at[n], cr.at[m], {"gx": beside_x[sx], "gy": beside_y[sy]}
        )

    def first_copy(s):
        n = tiles + 3
        return remote(
            rhs.at[face[s]], xin.at[0, 1 - s, 0], fs.at[s, n], fr.at[1 - s, n], {"gx": beside_x[s]}
        )

    def far_copy(s, t):
        return remote(
            coefs.at[1 + s, face[s], rows_of(t), :], far.at[1 - s, rows_of(t), :],
            fs.at[s, t], fr.at[1 - s, t], {"gx": beside_x[s]},
        )

    def far_edge_copy(s):
        return remote(
            far_corner.at[s], far_edge.at[1 - s], fs.at[s, tiles], fr.at[1 - s, tiles], {"gx": beside_x[s]}
        )

    def near_copies(s):
        device = {"gy": beside_y[s]}
        return (
            remote(own_row.at[s], near_row.at[1 - s], fs.at[s, tiles + 1], fr.at[1 - s, tiles + 1], device),
            remote(own_corner.at[s], near_corner.at[1 - s], fs.at[s, tiles + 2], fr.at[1 - s, tiles + 2], device),
        )

    def along_z(centre):
        lane = lax.broadcasted_iota(jnp.int32, centre.shape, 1)
        return (
            jnp.where(lane == 0, 0.0, pltpu.roll(centre, 1, 1)),
            jnp.where(lane == nz - 1, 0.0, pltpu.roll(centre, nz - 1, 1)),
        )

    def block_m(k, p, r, rows, low=True, high=True):
        here = slice(PAD + r, PAD + r + rows)
        mine = slice(r, r + rows)
        centre = fv[k, p, here, :]
        total = weight[0, p, mine, :] * centre
        if low:
            total = total + weight[1, p, mine, :] * fv[k, p - 1, here, :]
        if high:
            total = total + weight[2, p, mine, :] * fv[k, p + 1, here, :]
        total = total + weight[3, p, mine, :] * fv[k, p, PAD + r - 1 : PAD + r - 1 + rows, :]
        total = total + weight[4, p, mine, :] * fv[k, p, PAD + r + 1 : PAD + r + 1 + rows, :]
        minus_z, plus_z = along_z(centre)
        total = total + weight[5, p, mine, :] * minus_z
        total = total + weight[6, p, mine, :] * plus_z
        fw[k, p, here, :] = total
        return total

    def block_a(k, p, r, rows, minus_x=None, plus_x=None):
        here = slice(PAD + r, PAD + r + rows)
        mine = slice(r, r + rows)
        centre = fw[k, p, here, :]
        if minus_x is None:
            minus_x = fw[k, p - 1, here, :]
        if plus_x is None:
            plus_x = fw[k, p + 1, here, :]
        total = centre - weight[7, p, mine, :] * minus_x
        total = total - weight[8, p, mine, :] * plus_x
        total = total - weight[9, p, mine, :] * fw[k, p, PAD + r - 1 : PAD + r - 1 + rows, :]
        total = total - weight[10, p, mine, :] * fw[k, p, PAD + r + 1 : PAD + r + 1 + rows, :]
        minus_z, plus_z = along_z(centre)
        total = total - weight[11, p, mine, :] * minus_z
        total = total - weight[12, p, mine, :] * plus_z
        total = growth * (total - shifts[k] * fv[k, p, here, :])
        fv[k + 1, p, here, :] = total
        return total

    def face_m(k, s, t):
        total = block_m(k, face[s], t * TILE, TILE, low=s == 1, high=s == 0)
        xout[k, s, 1, rows_of(t), :] = total

    def face_a(k, s, t):
        rows = rows_of(t)
        here = slice(PAD + t * TILE, PAD + (t + 1) * TILE)
        beyond = xin[k, s, 1, rows, :] + far[s, rows, :] * fv[k, face[s], here, :]
        if s == 0:
            total = block_a(k, 0, t * TILE, TILE, minus_x=beyond)
        else:
            total = block_a(k, nx - 1, t * TILE, TILE, plus_x=beyond)
        xout[k + 1, s, 0, rows, :] = total

    def stage_corners(k, sy):
        row = PAD + edge[sy]
        for sx in range(2):
            cout[4 * k + 2 * sx + sy, :, :] = fv[k, face[sx], row : row + 1, :]

    def start_corners(k, sy):
        @pl.when(there[sy])
        def _():
            for sx in range(2):
                corner_copy(k, sx, sy).start()

    def stage_y(k, s, kind, fields):
        row = PAD + edge[s]
        for p in range(nx):
            yout[k, s, kind, p : p + 1, :] = fields[k, p, row : row + 1, :]

    def send_y(k, s):
        @pl.when(there[s])
        def _():
            stage_y(k, s, 0, fv)
            stage_y(k, s, 1, fw)
            y_copy(k, s).start()

    def own_edge(k, sy):
        row = PAD + edge[sy]
        yin[k, sy, 0, :, :] = own_row[sy] * yin[k, sy, 0, :, :]
        for p in range(nx):
            fw[k, p, row : row + 1, :] = fw[k, p, row : row + 1, :] + yin[k, sy, 0, p : p + 1, :]

    def finish_edge(k, sy):
        @pl.when(there[sy])
        def _():
            for sx in range(2):
                corner_copy(k, 1 - sx, 1 - sy).wait_recv()
            y_copy(k, 1 - sy).wait_recv()
            halo = PAD - 1 if sy == 0 else PAD + ny
            yin[k, sy, 1, :, :] = yin[k, sy, 1, :, :] + near_row[sy] * yout[k, sy, 0, :, :]
            for sx in range(2):
                p, q = face[sx], edge[sy]
                line = cin[4 * k + 2 * sx + sy, :, :]
                yin[k, sy, 1, p : p + 1, :] = yin[k, sy, 1, p : p + 1, :] + near_corner[sy, sx : sx + 1, :] * line
                xin[k, sx, 1, q : q + 1, :] = xin[k, sx, 1, q : q + 1, :] + far_edge[sx, sy : sy + 1, :] * line
            own_edge(k, sy)
            for p in range(nx):
                fw[k, p, halo : halo + 1, :] = yin[k, sy, 1, p : p + 1, :]

    def products(i, planes, start, size):
        def add(p, totals):
            a = fv[i, p, pl.ds(PAD + start, size), :]
            return tuple(
                total + jnp.sum((a * fv[j, p, pl.ds(PAD + start, size), :]).reshape(size // 8, 8, nz), axis=0)
                for j, total in enumerate(totals)
            )

        totals = lax.fori_loop(*planes, add, tuple(sums[j] for j in range(i + 1)))
        for j, total in enumerate(totals):
            sums[j, :, :] = total

    def forget(i):
        for j in range(i + 1):
            sums[j, :, :] = jnp.zeros((8, nz), jnp.float32)

    def keep(i):
        for j in range(i + 1):
            row = jnp.sum(sums[j], axis=0, keepdims=True)
            flat = row[:, :ROWS]
            for q in range(1, nz // ROWS):
                flat = flat + row[:, q * ROWS : (q + 1) * ROWS]
            n = i * (i + 1) // 2 + j
            part[n : n + 1, :] = flat

    def inner_rows():
        return [(r, min(16, ny - TILE - r)) for r in range(TILE, ny - TILE, 16)]

    def inner_m(k):
        def one(p, c):
            for r, rows in inner_rows():
                block_m(k, p, r, rows)
            return c

        lax.fori_loop(1, nx - 1, one, 0)

    def inner_a(k):
        def one(p, c):
            for r, rows in inner_rows():
                block_a(k, p, r, rows)
            return c

        lax.fori_loop(2, nx - 2, one, 0)

    def edge_m(k, sy):
        def one(p, c):
            block_m(k, p, (0, ny - TILE)[sy], TILE)
            return c

        lax.fori_loop(1, nx - 1, one, 0)

    def edge_a(k, sy):
        def one(p, c):
            block_a(k, p, (0, ny - TILE)[sy], TILE)
            return c

        lax.fori_loop(2, nx - 2, one, 0)

    sequence = middle_out(tiles)


    loads[0].wait()
    for sy in range(2):
        stage_corners(0, sy)
    pl.semaphore_wait(barrier, greetings)
    for s in range(2):
        first_copy(s).start()
    for s in range(2):
        start_corners(0, s)
    if strides:
        hello_signal(0)
    loads[1].wait()
    loads[2].wait()
    for t in sequence:
        for s in range(2):
            face_m(0, s, t)
            x_copy(0, s, t).start()
            far_copy(s, t).start()
    for s in range(2):
        for sy in range(2):
            far_corner[s, sy : sy + 1, :] = weight[3 + sy, face[s], edge[sy] : edge[sy] + 1, :]
        far_edge_copy(s).start()
    loads[3].wait()
    for s in range(2):
        r = edge[s]
        for p in range(nx):
            own_row[s, p : p + 1, :] = weight[3 + s, p, r : r + 1, :]
        for sx in range(2):
            own_corner[s, sx : sx + 1, :] = weight[1 + sx, face[sx], r : r + 1, :]

        @pl.when(there[s])
        def _():
            for copy in near_copies(s):
                copy.start()

        edge_m(0, s)
        send_y(0, s)
    inner_m(0)
    loads[4].wait()
    loads[5].wait()

    def step(k, send):
        inner_a(k)
        forget(k)
        products(k, (0, nx), 0, ny)
        keep(k)
        hello_rounds(k)
        if not send:
            forget(k + 1)
            products(k + 1, (2, nx - 2), TILE, ny - 2 * TILE)
        arrived, final = set(), set()

        def needs(u):
            return {q for q in (u - 1, u, u + 1) if 0 <= q < tiles}

        for t in sequence:
            sides = [1, 0] if t == sequence[-1] else []
            here = slice(PAD + t * TILE, PAD + (t + 1) * TILE)
            for s in range(2):
                x_copy(k, 1 - s, t).wait_recv()
                if k == 0:
                    if t == sequence[0]:
                        first_copy(1 - s).wait_recv()
                    far_copy(1 - s, t).wait_recv()
                fw[k, face[s], here, :] = (
                    fw[k, face[s], here, :] + weight[1 + s, face[s], rows_of(t), :] * xin[k, s, 0, rows_of(t), :]
                )
            arrived.add(t)
            for sy in sides:
                if k == 0 and sy == sides[0]:
                    for s in range(2):
                        far_edge_copy(1 - s).wait_recv()
                if k == 0:

                    @pl.when(there[sy])
                    def _():
                        for copy in near_copies(1 - sy):
                            copy.wait_recv()

                finish_edge(k, sy)
            ready = [
                u for u in sequence
                if u not in final and needs(u) <= arrived and (sides or 0 < u < tiles - 1)
            ]
            for u in ready:
                final.add(u)
            extra = sorted(set().union(*[needs(u) for u in ready]) - final) if send and ready else []
            for u in ready + extra:
                for s in range(2):
                    face_a(k, s, u)
            for u in ready:
                block_a(k, 1, u * TILE, TILE)
                block_a(k, nx - 2, u * TILE, TILE)
            if send:
                for sy in sides:
                    stage_corners(k + 1, sy)
                    start_corners(k + 1, sy)
                for u in ready:
                    for s in range(2):
                        face_m(k + 1, s, u)
                        x_copy(k + 1, s, u).start()
            for sy in sides:
                edge_a(k, sy)
                if send:
                    edge_m(k + 1, sy)
                    send_y(k + 1, sy)
                else:
                    products(k + 1, (2, nx - 2), (0, ny - TILE)[sy], TILE)
        if send:
            inner_m(k + 1)

    for k in range(steps):
        step(k, k + 1 < steps)
    products(steps, (0, 2), 0, ny)
    products(steps, (nx - 2, nx), 0, ny)
    keep(steps)

    height = part.shape[0]
    row = lax.broadcasted_iota(jnp.int32, (height, ROWS), 0)
    lane = lax.broadcasted_iota(jnp.int32, (height, ROWS), 1)
    column = jnp.sum(part[...], axis=1, keepdims=True)
    packed = jnp.sum(jnp.where(row == lane, jnp.broadcast_to(column, row.shape), 0.0), axis=0, keepdims=True)
    peers[pl.ds(me, 1), :] = packed

    low_half = gx < n_gx // 2

    def peer_copy(j):
        down, up = count - 1 - j, j
        other = jnp.where(low_half, jnp.where(down > me, down, down - 1), jnp.where(up < me, up, up + 1))
        device = {"gx": lax.div(other, n_gy), "gy": lax.rem(other, n_gy)}
        return remote(peers.at[pl.ds(me, 1), :], peers.at[pl.ds(me, 1), :], gs.at[0], gr.at[0], device)

    for j in range(count - 1):
        peer_copy(j).start()

    def all_peers():
        rows = pl.ds(0, count - 1)
        return remote(peers.at[rows, :], peers.at[rows, :], gs.at[0], gr.at[0], peer(1))

    for k in range(steps):
        for s in range(2):
            for t in range(tiles):
                x_copy(k, s, t).wait_send()

            @pl.when(there[s])
            def _():
                y_copy(k, s).wait_send()
                for sx in range(2):
                    corner_copy(k, sx, s).wait_send()

    for s in range(2):
        first_copy(s).wait_send()
        for t in range(tiles):
            far_copy(s, t).wait_send()
        far_edge_copy(s).wait_send()

        @pl.when(there[s])
        def _():
            for copy in near_copies(s):
                copy.wait_send()

    all_peers().wait_recv()
    total = jnp.sum(peers[...], axis=0, keepdims=True)
    spread = jnp.sum(jnp.where(row == lane, jnp.broadcast_to(total, row.shape), 0.0), axis=1, keepdims=True)
    gram[0:height, :] = jnp.broadcast_to(spread, row.shape)
    for k in range(steps):
        gram[height + k : height + k + 1, :] = jnp.full((1, ROWS), shifts[k], jnp.float32)
    all_peers().wait_send()


def small_algebra(gram, steps, cells):
    order = steps + 1
    height = -(-(order * (order + 1) // 2) // 8) * 8
    shifts = [gram[height + k : height + k + 1, :] for k in range(steps)]
    sums = gram[:height] / cells

    def entry(i, j):
        n = max(i, j) * (max(i, j) + 1) // 2 + min(i, j)
        return sums[n : n + 1, :]

    factor = {}
    for i in range(order):
        value = entry(i, i)
        for k in range(i):
            value = value - factor[k, i] * factor[k, i]
        factor[i, i] = jnp.sqrt(value)
        for j in range(i + 1, order):
            value = entry(i, j)
            for k in range(i):
                value = value - factor[k, i] * factor[k, j]
            factor[i, j] = value / factor[i, i]
    inverse = {}
    for j in range(order):
        inverse[j, j] = 1.0 / factor[j, j]
        for i in range(j - 1, -1, -1):
            value = factor[i, i + 1] * inverse[i + 1, j]
            for k in range(i + 2, j + 1):
                value = value + factor[i, k] * inverse[k, j]
            inverse[i, j] = -value / factor[i, i]
    zero = jnp.zeros_like(factor[0, 0])

    def upper(i, j):
        return factor.get((i, j), zero)

    hess = [[upper(i, k) * shifts[k] + upper(i, k + 1) * (1.0 / growth) for k in range(steps)] for i in range(order)]
    target = [upper(i, 0) for i in range(order)]
    for k in range(steps):
        top, below = hess[k][k], hess[k + 1][k]
        radius = jnp.sqrt(top * top + below * below)
        cosine, sine = top / radius, below / radius
        for c in range(k, steps):
            a, b = hess[k][c], hess[k + 1][c]
            hess[k][c] = cosine * a + sine * b
            hess[k + 1][c] = cosine * b - sine * a
        a, b = target[k], target[k + 1]
        target[k] = cosine * a + sine * b
        target[k + 1] = cosine * b - sine * a
    weights = [None] * steps
    for i in range(steps - 1, -1, -1):
        value = target[i]
        for k in range(i + 1, steps):
            value = value - hess[i][k] * weights[k]
        weights[i] = value / hess[i][i]
    combine = []
    for j in range(order):
        value = zero + (1.0 if j == 0 else 0.0)
        if j < steps:
            value = value - shifts[j] * weights[j]
        if j > 0:
            value = value - (1.0 / growth) * weights[j - 1]
        combine.append(value)
    return factor, inverse, weights, combine


def combine_kernel(cells, gram, v, w, basis, factor_out, solution_out, residual, table, basis_v, sol_v, res_v, factor_v, sem, factor_sem):
    order, nx, ny, nz = basis_v.shape
    steps = order - 1
    pairs = [(j, k) for k in range(order) for j in range(k + 1)]
    tail = len(pairs)

    factor, inverse, weights, combine = small_algebra(gram[...], steps, cells)
    values = [inverse[p] for p in pairs] + weights + combine
    for n, value in enumerate(values):
        table[n] = jnp.broadcast_to(value, table.shape[1:])
    row = lax.broadcasted_iota(jnp.int32, (8, ROWS), 0)
    column = lax.broadcasted_iota(jnp.int32, (8, ROWS), 1)
    whole = jnp.zeros((8, ROWS), jnp.float32)
    for (i, j), value in factor.items():
        whole = jnp.where((row == i) & (column == j), value, whole)
    factor_v[...] = whole[:order, :order]
    factor_copy = pltpu.make_async_copy(factor_v, factor_out, factor_sem)
    factor_copy.start()

    def mul(n, x):
        return table[n][None] * x

    deep = 16 if ny % 16 == 0 else 8

    def tile(p, t):
        rows = pl.ds(pl.multiple_of(t * deep, deep), deep)
        for q in range(0, nz, ROWS):
            lanes = slice(q, q + ROWS)
            load = lambda x: x.reshape(deep // 8, 8, ROWS)
            padded = pl.ds(pl.multiple_of(PAD + t * deep, 8), deep)
            fields = [load(v[k, p, padded, lanes]) for k in range(order)]
            for k in range(order):
                total = None
                for j in range(k + 1):
                    term = mul(pairs.index((j, k)), fields[j])
                    total = term if total is None else total + term
                basis_v[k, p, rows, lanes] = total.reshape(deep, ROWS)
            total = mul(tail, load(w[0, p, padded, lanes]))
            for k in range(1, steps):
                total = total + mul(tail + k, load(w[k, p, padded, lanes]))
            sol_v[p, rows, lanes] = total.reshape(deep, ROWS)
            total = mul(tail + steps, fields[0])
            for j in range(1, order):
                total = total + mul(tail + steps + j, fields[j])
            res_v[p, rows, lanes] = total.reshape(deep, ROWS)

    def copies(p):
        return (
            pltpu.make_async_copy(basis_v.at[:, p], basis.at[:, p], sem.at[p, 0]),
            pltpu.make_async_copy(sol_v.at[p], solution_out.at[p], sem.at[p, 1]),
            pltpu.make_async_copy(res_v.at[p], residual.at[p], sem.at[p, 2]),
        )

    def plane(p, c):
        def inner(t, d):
            tile(p, t)
            return d

        lax.fori_loop(0, ny // deep, inner, 0)
        for copy in copies(p):
            copy.start()
        return c

    def finish(p, c):
        for copy in copies(p):
            copy.wait()
        return c

    lax.fori_loop(0, nx, plane, 0)
    lax.fori_loop(0, nx, finish, 0)
    factor_copy.wait()


def device_body(n_gx, n_gy, rhs, coefs, shifts):
    steps = shifts.shape[0]
    order = steps + 1
    nx, ny, nz = rhs.shape
    f32 = jnp.float32
    grown = (nx, ny + 2 * PAD, nz)
    height = -(-(order * (order + 1) // 2) // 8) * 8
    gram_rows = height + -(-steps // 8) * 8
    tiles = ny // TILE
    hbm = pl.BlockSpec(memory_space=pltpu.HBM)
    vmem = pl.BlockSpec(memory_space=pltpu.VMEM)
    dma = pltpu.SemaphoreType.DMA
    rhs = pltpu.with_memory_space_constraint(rhs, pltpu.HBM)
    coefs = pltpu.with_memory_space_constraint(coefs, pltpu.HBM)
    shifts = pltpu.with_memory_space_constraint(shifts, pltpu.HBM)
    v, w, gram = pl.pallas_call(
        functools.partial(basis_kernel, n_gx, n_gy),
        out_shape=(
            jax.ShapeDtypeStruct((order,) + grown, f32),
            jax.ShapeDtypeStruct((steps,) + grown, f32),
            jax.ShapeDtypeStruct((gram_rows, ROWS), f32),
        ),
        in_specs=[hbm, hbm, hbm],
        out_specs=(vmem, vmem, vmem),
        scratch_shapes=[
            pltpu.VMEM(coefs.shape, f32),
            pltpu.VMEM((height, ROWS), f32),
            pltpu.VMEM((order, 8, nz), f32),
            pltpu.VMEM((n_gx * n_gy, ROWS), f32),
            pltpu.SMEM(shifts.shape, f32),
            pltpu.VMEM((order, 2, 2, ny, nz), f32),
            pltpu.VMEM((steps, 2, 2, ny, nz), f32),
            pltpu.VMEM((order, 2, 2, nx, nz), f32),
            pltpu.VMEM((steps, 2, 2, nx, nz), f32),
            pltpu.VMEM((4 * order, 1, nz), f32),
            pltpu.VMEM((4 * steps, 1, nz), f32),
            pltpu.VMEM((2, ny, nz), f32),
            pltpu.VMEM((2, 2, nz), f32),
            pltpu.VMEM((2, nx, nz), f32),
            pltpu.VMEM((2, 2, nz), f32),
            pltpu.VMEM((2, nx, nz), f32),
            pltpu.VMEM((2, 2, nz), f32),
            pltpu.VMEM((2, 2, nz), f32),
            dma((6,)),
            pltpu.SemaphoreType.REGULAR((16,)),
            dma((2 * steps * tiles,)),
            dma((2 * steps * tiles,)),
            dma((2 * steps,)),
            dma((2 * steps,)),
            dma((4 * steps,)),
            dma((4 * steps,)),
            dma((2, 2 * tiles + 3)),
            dma((2, 2 * tiles + 3)),
            dma((1,)),
            dma((1,)),
        ],
        compiler_params=pltpu.CompilerParams(
            collective_id=0, has_side_effects=True, vmem_limit_bytes=32 * 2**20
        ),
        name="basis",
    )(shifts, rhs, coefs)

    cells = float(nx * ny * nz * n_gx * n_gy)
    return pl.pallas_call(
        functools.partial(combine_kernel, cells),
        out_shape=(
            jax.ShapeDtypeStruct((order, nx, ny, nz), f32),
            jax.ShapeDtypeStruct((order, order), f32),
            jax.ShapeDtypeStruct((nx, ny, nz), f32),
            jax.ShapeDtypeStruct((nx, ny, nz), f32),
        ),
        in_specs=[vmem, vmem, vmem],
        out_specs=(hbm, hbm, hbm, hbm),
        scratch_shapes=[
            pltpu.VMEM((order * (order + 1) // 2 + steps + order, 8, ROWS), f32),
            pltpu.VMEM((order, nx, ny, nz), f32),
            pltpu.VMEM((nx, ny, nz), f32),
            pltpu.VMEM((nx, ny, nz), f32),
            pltpu.VMEM((order, order), f32),
            dma((nx, 3)),
            dma,
        ],
        compiler_params=pltpu.CompilerParams(vmem_limit_bytes=32 * 2**20),
        name="combine",
    )(gram, v, w)


def solution(mesh):
    placed = (P("gx", "gy", None), P(None, "gx", "gy", None), P())
    return jax.shard_map(
        functools.partial(device_body, mesh.shape["gx"], mesh.shape["gy"]),
        mesh=mesh,
        in_specs=placed,
        out_specs=(P(None, "gx", "gy", None), P(), P("gx", "gy", None), P("gx", "gy", None)),
        check_vma=False,
    )
```

```python
import functools

import jax
import jax.numpy as jnp
from jax import lax
from jax.experimental import pallas as pl
from jax.experimental.pallas import tpu as pltpu
from jax.sharding import PartitionSpec as P

growth = 2.0
MESH = pl.DeviceIdType.MESH
PAD = 8
ROWS = 128
TILE = 8


def middle_out(count):
    low, high = (count - 1) // 2, (count - 1) // 2 + 1
    order = []
    while low >= 0 or high < count:
        if high < count:
            order.append(high)
            high += 1
        if low >= 0:
            order.append(low)
            low -= 1
    return order


def basis_kernel(
    n_gx, n_gy, shifts_hbm, rhs, coefs, fv, fw, gram,
    weight, part, sums, peers, shifts, xout, xin, yout, yin, cout, cin,
    far, far_corner, own_row, own_corner, near_row, near_corner, far_edge,
    load_sem, hello, xs, xr, ys, yr, cs, cr, fs, fr, gs, gr,
):
    steps = shifts.shape[0]
    order = steps + 1
    nx, ny, nz = rhs.shape
    tiles = ny // TILE
    assert tiles >= 4 and nx >= 4 and ny % TILE == 0
    body = slice(PAD, PAD + ny)
    face = (0, nx - 1)
    edge = (0, ny - 1)
    gx, gy = lax.axis_index("gx"), lax.axis_index("gy")
    beside_x = (lax.rem(gx + n_gx - 1, n_gx), lax.rem(gx + 1, n_gx))
    beside_y = (jnp.maximum(gy - 1, 0), jnp.minimum(gy + 1, n_gy - 1))
    there = (gy > 0, gy < n_gy - 1)
    count = n_gx * n_gy
    me = gx * n_gy + gy

    loads = [
        pltpu.make_async_copy(rhs, fv.at[0, :, body, :], load_sem.at[0]),
        pltpu.make_async_copy(coefs.at[0:7, 0], weight.at[0:7, 0], load_sem.at[1]),
        pltpu.make_async_copy(coefs.at[0:7, nx - 1], weight.at[0:7, nx - 1], load_sem.at[2]),
        pltpu.make_async_copy(coefs.at[0:7, 1 : nx - 1], weight.at[0:7, 1 : nx - 1], load_sem.at[3]),
        pltpu.make_async_copy(coefs.at[7:13], weight.at[7:13], load_sem.at[4]),
        pltpu.make_async_copy(shifts_hbm, shifts, load_sem.at[5]),
    ]
    cin[...] = jnp.zeros_like(cin)

    barrier = pltpu.get_barrier_semaphore()

    def peer(d):
        other = lax.rem(me + d, count)
        return {"gx": lax.div(other, n_gy), "gy": lax.rem(other, n_gy)}

    def greet(device):
        pl.semaphore_signal(barrier, inc=1, device_id=device, device_id_type=MESH)

    for x in beside_x:
        greet({"gx": x})
    for s in range(2):

        @pl.when(there[s])
        def _():
            greet({"gy": beside_y[s]})
            for x in beside_x:
                greet({"gx": x, "gy": beside_y[s]})

    greet(peer(1))
    greet(peer(count - 1))
    for load in loads:
        load.start()
    greetings = 4 + 3 * (there[0].astype(jnp.int32) + there[1].astype(jnp.int32))

    strides = []
    while (2 ** len(strides)) * 2 < count:
        strides.append(2 ** len(strides))

    def hello_signal(r):
        for d in (strides[r], count - strides[r]):
            pl.semaphore_signal(hello.at[r], inc=1, device_id=peer(d), device_id_type=MESH)

    def hello_rounds(k):
        share = -(-len(strides) // steps)
        for r in range(k * share, min((k + 1) * share, len(strides))):
            pl.semaphore_wait(hello.at[r], 2)
            if r + 1 < len(strides):
                hello_signal(r + 1)

    part[...] = jnp.zeros_like(part)
    blank = jnp.zeros((PAD, nz), jnp.float32)
    for fields in (fv, fw):

        def clear(p, c):
            for k in range(fields.shape[0]):
                fields[k, p, 0:PAD, :] = blank
                fields[k, p, PAD + ny : PAD + ny + PAD, :] = blank
            return c

        lax.fori_loop(0, nx, clear, 0)

    def rows_of(t):
        return slice(t * TILE, (t + 1) * TILE)

    def remote(source, target, send, receive, device):
        return pltpu.make_async_remote_copy(
            src_ref=source, dst_ref=target, send_sem=send, recv_sem=receive,
            device_id=device, device_id_type=MESH,
        )

    def x_copy(k, s, t):
        n, m = (2 * k + s) * tiles + t, (2 * k + 1 - s) * tiles + t
        kinds = slice(1 if k == 0 else 0, 2)
        return remote(
            xout.at[k, s, kinds, rows_of(t), :], xin.at[k, 1 - s, kinds, rows_of(t), :],
            xs.at[n], xr.at[m], {"gx": beside_x[s]},
        )

    def y_copy(k, s):
        return remote(
            yout.at[k, s], yin.at[k, 1 - s], ys.at[2 * k + s], yr.at[2 * k + 1 - s], {"gy": beside_y[s]}
        )

    def corner_copy(k, sx, sy):
        n, m = 4 * k + 2 * sx + sy, 4 * k + 2 * (1 - sx) + 1 - sy
        return remote(
            cout.at[n], cin.at[m], cs.at[n], cr.at[m], {"gx": beside_x[sx], "gy": beside_y[sy]}
        )

    def first_copy(s):
        n = tiles + 3
        return remote(
            rhs.at[face[s]], xin.at[0, 1 - s, 0], fs.at[s, n], fr.at[1 - s, n], {"gx": beside_x[s]}
        )

    def far_copy(s, t):
        return remote(
            coefs.at[1 + s, face[s], rows_of(t), :], far.at[1 - s, rows_of(t), :],
            fs.at[s, t], fr.at[1 - s, t], {"gx": beside_x[s]},
        )

    def far_edge_copy(s):
        return remote(
            far_corner.at[s], far_edge.at[1 - s], fs.at[s, tiles], fr.at[1 - s, tiles], {"gx": beside_x[s]}
        )

    def near_copies(s):
        device = {"gy": beside_y[s]}
        return (
            remote(own_row.at[s], near_row.at[1 - s], fs.at[s, tiles + 1], fr.at[1 - s, tiles + 1], device),
            remote(own_corner.at[s], near_corner.at[1 - s], fs.at[s, tiles + 2], fr.at[1 - s, tiles + 2], device),
        )

    def along_z(centre):
        lane = lax.broadcasted_iota(jnp.int32, centre.shape, 1)
        return (
            jnp.where(lane == 0, 0.0, pltpu.roll(centre, 1, 1)),
            jnp.where(lane == nz - 1, 0.0, pltpu.roll(centre, nz - 1, 1)),
        )

    def block_m(k, p, r, rows, low=True, high=True):
        here = slice(PAD + r, PAD + r + rows)
        mine = slice(r, r + rows)
        centre = fv[k, p, here, :]
        total = weight[0, p, mine, :] * centre
        if low:
            total = total + weight[1, p, mine, :] * fv[k, p - 1, here, :]
        if high:
            total = total + weight[2, p, mine, :] * fv[k, p + 1, here, :]
        total = total + weight[3, p, mine, :] * fv[k, p, PAD + r - 1 : PAD + r - 1 + rows, :]
        total = total + weight[4, p, mine, :] * fv[k, p, PAD + r + 1 : PAD + r + 1 + rows, :]
        minus_z, plus_z = along_z(centre)
        total = total + weight[5, p, mine, :] * minus_z
        total = total + weight[6, p, mine, :] * plus_z
        fw[k, p, here, :] = total
        return total

    def block_a(k, p, r, rows, minus_x=None, plus_x=None):
        here = slice(PAD + r, PAD + r + rows)
        mine = slice(r, r + rows)
        centre = fw[k, p, here, :]
        if minus_x is None:
            minus_x = fw[k, p - 1, here, :]
        if plus_x is None:
            plus_x = fw[k, p + 1, here, :]
        total = centre - weight[7, p, mine, :] * minus_x
        total = total - weight[8, p, mine, :] * plus_x
        total = total - weight[9, p, mine, :] * fw[k, p, PAD + r - 1 : PAD + r - 1 + rows, :]
        total = total - weight[10, p, mine, :] * fw[k, p, PAD + r + 1 : PAD + r + 1 + rows, :]
        minus_z, plus_z = along_z(centre)
        total = total - weight[11, p, mine, :] * minus_z
        total = total - weight[12, p, mine, :] * plus_z
        total = growth * (total - shifts[k] * fv[k, p, here, :])
        fv[k + 1, p, here, :] = total
        return total

    def face_m(k, s, t):
        total = block_m(k, face[s], t * TILE, TILE, low=s == 1, high=s == 0)
        xout[k, s, 1, rows_of(t), :] = total

    def face_a(k, s, t):
        rows = rows_of(t)
        here = slice(PAD + t * TILE, PAD + (t + 1) * TILE)
        beyond = xin[k, s, 1, rows, :] + far[s, rows, :] * fv[k, face[s], here, :]
        if s == 0:
            total = block_a(k, 0, t * TILE, TILE, minus_x=beyond)
        else:
            total = block_a(k, nx - 1, t * TILE, TILE, plus_x=beyond)
        xout[k + 1, s, 0, rows, :] = total

    def stage_corners(k, sy):
        row = PAD + edge[sy]
        for sx in range(2):
            cout[4 * k + 2 * sx + sy, :, :] = fv[k, face[sx], row : row + 1, :]

    def start_corners(k, sy):
        @pl.when(there[sy])
        def _():
            for sx in range(2):
                corner_copy(k, sx, sy).start()

    def stage_y(k, s, kind, fields):
        row = PAD + edge[s]
        for p in range(nx):
            yout[k, s, kind, p : p + 1, :] = fields[k, p, row : row + 1, :]

    def send_y(k, s):
        @pl.when(there[s])
        def _():
            stage_y(k, s, 0, fv)
            stage_y(k, s, 1, fw)
            y_copy(k, s).start()

    def own_edge(k, sy):
        row = PAD + edge[sy]
        yin[k, sy, 0, :, :] = own_row[sy] * yin[k, sy, 0, :, :]
        for p in range(nx):
            fw[k, p, row : row + 1, :] = fw[k, p, row : row + 1, :] + yin[k, sy, 0, p : p + 1, :]

    def finish_edge(k, sy):
        @pl.when(there[sy])
        def _():
            for sx in range(2):
                corner_copy(k, 1 - sx, 1 - sy).wait_recv()
            y_copy(k, 1 - sy).wait_recv()
            halo = PAD - 1 if sy == 0 else PAD + ny
            yin[k, sy, 1, :, :] = yin[k, sy, 1, :, :] + near_row[sy] * yout[k, sy, 0, :, :]
            for sx in range(2):
                p, q = face[sx], edge[sy]
                line = cin[4 * k + 2 * sx + sy, :, :]
                yin[k, sy, 1, p : p + 1, :] = yin[k, sy, 1, p : p + 1, :] + near_corner[sy, sx : sx + 1, :] * line
                xin[k, sx, 1, q : q + 1, :] = xin[k, sx, 1, q : q + 1, :] + far_edge[sx, sy : sy + 1, :] * line
            own_edge(k, sy)
            for p in range(nx):
                fw[k, p, halo : halo + 1, :] = yin[k, sy, 1, p : p + 1, :]

    def products(i, planes, start, size):
        def add(p, totals):
            a = fv[i, p, pl.ds(PAD + start, size), :]
            return tuple(
                total + jnp.sum((a * fv[j, p, pl.ds(PAD + start, size), :]).reshape(size // 8, 8, nz), axis=0)
                for j, total in enumerate(totals)
            )

        totals = lax.fori_loop(*planes, add, tuple(sums[j] for j in range(i + 1)))
        for j, total in enumerate(totals):
            sums[j, :, :] = total

    def forget(i):
        for j in range(i + 1):
            sums[j, :, :] = jnp.zeros((8, nz), jnp.float32)

    def keep(i):
        for j in range(i + 1):
            row = jnp.sum(sums[j], axis=0, keepdims=True)
            flat = row[:, :ROWS]
            for q in range(1, nz // ROWS):
                flat = flat + row[:, q * ROWS : (q + 1) * ROWS]
            n = i * (i + 1) // 2 + j
            part[n : n + 1, :] = flat

    def inner_rows():
        return [(r, min(16, ny - TILE - r)) for r in range(TILE, ny - TILE, 16)]

    def inner_m(k):
        def one(p, c):
            for r, rows in inner_rows():
                block_m(k, p, r, rows)
            return c

        lax.fori_loop(1, nx - 1, one, 0)

    def inner_a(k):
        def one(p, c):
            for r, rows in inner_rows():
                block_a(k, p, r, rows)
            return c

        lax.fori_loop(2, nx - 2, one, 0)

    def edge_m(k, sy):
        def one(p, c):
            block_m(k, p, (0, ny - TILE)[sy], TILE)
            return c

        lax.fori_loop(1, nx - 1, one, 0)

    def edge_a(k, sy):
        def one(p, c):
            block_a(k, p, (0, ny - TILE)[sy], TILE)
            return c

        lax.fori_loop(2, nx - 2, one, 0)

    sequence = middle_out(tiles)


    pl.semaphore_wait(barrier, greetings)
    for s in range(2):
        first_copy(s).start()
    loads[0].wait()
    for sy in range(2):
        stage_corners(0, sy)
    for s in range(2):
        start_corners(0, s)
    if strides:
        hello_signal(0)
    loads[1].wait()
    loads[2].wait()
    for s in range(2):
        for sy in range(2):
            far_corner[s, sy : sy + 1, :] = weight[3 + sy, face[s], edge[sy] : edge[sy] + 1, :]
        far_edge_copy(s).start()
    for t in sequence:
        for s in range(2):
            face_m(0, s, t)
            x_copy(0, s, t).start()
            far_copy(s, t).start()
    loads[3].wait()
    for s in range(2):
        r = edge[s]
        for p in range(nx):
            own_row[s, p : p + 1, :] = weight[3 + s, p, r : r + 1, :]
        for sx in range(2):
            own_corner[s, sx : sx + 1, :] = weight[1 + sx, face[sx], r : r + 1, :]

        @pl.when(there[s])
        def _():
            for copy in near_copies(s):
                copy.start()

        edge_m(0, s)
        send_y(0, s)
    inner_m(0)
    loads[4].wait()
    loads[5].wait()

    final_at = (sequence[-1], sequence[-1])

    def step(k, send):
        inner_a(k)
        forget(k)
        products(k, (0, nx), 0, ny)
        keep(k)
        hello_rounds(k)
        if not send:
            forget(k + 1)
            products(k + 1, (2, nx - 2), TILE, ny - 2 * TILE)
        arrived, final = set(), set()

        def needs(u):
            return {q for q in (u - 1, u, u + 1) if 0 <= q < tiles}

        def advance(ready, corners):
            final.update(ready)
            drafts = sorted(set().union(*[needs(u) for u in ready]) - final) if send else []
            for s in range(2):
                for u in ready + drafts:
                    face_a(k, s, u)
            for u in ready:
                for s in range(2):
                    block_a(k, (1, nx - 2)[s], u * TILE, TILE)
            if send:
                for sy in corners:
                    stage_corners(k + 1, sy)
                    start_corners(k + 1, sy)
                for u in ready:
                    for s in range(2):
                        face_m(k + 1, s, u)
                        x_copy(k + 1, s, u).start()

        for t in sequence:
            here = slice(PAD + t * TILE, PAD + (t + 1) * TILE)
            for s in range(2):
                x_copy(k, 1 - s, t).wait_recv()
                if k == 0:
                    if t == sequence[0]:
                        first_copy(1 - s).wait_recv()
                    far_copy(1 - s, t).wait_recv()
                fw[k, face[s], here, :] = (
                    fw[k, face[s], here, :] + weight[1 + s, face[s], rows_of(t), :] * xin[k, s, 0, rows_of(t), :]
                )
            arrived.add(t)
            ready = [u for u in sequence if u not in final and needs(u) <= arrived and 0 < u < tiles - 1]
            ends = [sy for sy in (1, 0) if t == final_at[sy]]
            for sy in ends:
                if k == 0:
                    if sy == 1:
                        for s in range(2):
                            far_edge_copy(1 - s).wait_recv()

                    @pl.when(there[sy])
                    def _():
                        for copy in near_copies(1 - sy):
                            copy.wait_recv()

                finish_edge(k, sy)
                ready.append((0, tiles - 1)[sy])
            if ready:
                advance(ready, ends)
            if not send and t == sequence[-2]:
                for planes in ((0, 2), (nx - 2, nx)):
                    products(k + 1, planes, 2 * TILE, ny - 4 * TILE)
        for sy in (1, 0):
            edge_a(k, sy)
            if send:
                edge_m(k + 1, sy)
                send_y(k + 1, sy)
            else:
                products(k + 1, (2, nx - 2), (0, ny - TILE)[sy], TILE)
        if send:
            inner_m(k + 1)

    for k in range(steps):
        step(k, k + 1 < steps)
    for planes in ((0, 2), (nx - 2, nx)):
        for start in (0, ny - 2 * TILE):
            products(steps, planes, start, 2 * TILE)
    keep(steps)

    height = part.shape[0]
    row = lax.broadcasted_iota(jnp.int32, (height, ROWS), 0)
    lane = lax.broadcasted_iota(jnp.int32, (height, ROWS), 1)
    column = jnp.sum(part[...], axis=1, keepdims=True)
    packed = jnp.sum(jnp.where(row == lane, jnp.broadcast_to(column, row.shape), 0.0), axis=0, keepdims=True)
    peers[pl.ds(me, 1), :] = packed

    low_half = gx < n_gx // 2

    def peer_copy(j):
        down, up = count - 1 - j, j
        other = jnp.where(low_half, jnp.where(down > me, down, down - 1), jnp.where(up < me, up, up + 1))
        device = {"gx": lax.div(other, n_gy), "gy": lax.rem(other, n_gy)}
        return remote(peers.at[pl.ds(me, 1), :], peers.at[pl.ds(me, 1), :], gs.at[0], gr.at[0], device)

    for j in range(count - 1):
        peer_copy(j).start()

    def all_peers():
        rows = pl.ds(0, count - 1)
        return remote(peers.at[rows, :], peers.at[rows, :], gs.at[0], gr.at[0], peer(1))

    for k in range(steps):
        for s in range(2):
            for t in range(tiles):
                x_copy(k, s, t).wait_send()

            @pl.when(there[s])
            def _():
                y_copy(k, s).wait_send()
                for sx in range(2):
                    corner_copy(k, sx, s).wait_send()

    for s in range(2):
        first_copy(s).wait_send()
        for t in range(tiles):
            far_copy(s, t).wait_send()
        far_edge_copy(s).wait_send()

        @pl.when(there[s])
        def _():
            for copy in near_copies(s):
                copy.wait_send()

    all_peers().wait_recv()
    total = jnp.sum(peers[...], axis=0, keepdims=True)
    spread = jnp.sum(jnp.where(row == lane, jnp.broadcast_to(total, row.shape), 0.0), axis=1, keepdims=True)
    gram[0:height, :] = jnp.broadcast_to(spread, row.shape)
    for k in range(steps):
        gram[height + k : height + k + 1, :] = jnp.full((1, ROWS), shifts[k], jnp.float32)
    all_peers().wait_send()


def small_algebra(gram, steps, cells):
    order = steps + 1
    height = -(-(order * (order + 1) // 2) // 8) * 8
    shifts = [gram[height + k : height + k + 1, :] for k in range(steps)]
    sums = gram[:height] / cells

    def entry(i, j):
        n = max(i, j) * (max(i, j) + 1) // 2 + min(i, j)
        return sums[n : n + 1, :]

    factor = {}
    for i in range(order):
        value = entry(i, i)
        for k in range(i):
            value = value - factor[k, i] * factor[k, i]
        factor[i, i] = jnp.sqrt(value)
        for j in range(i + 1, order):
            value = entry(i, j)
            for k in range(i):
                value = value - factor[k, i] * factor[k, j]
            factor[i, j] = value / factor[i, i]
    inverse = {}
    for j in range(order):
        inverse[j, j] = 1.0 / factor[j, j]
        for i in range(j - 1, -1, -1):
            value = factor[i, i + 1] * inverse[i + 1, j]
            for k in range(i + 2, j + 1):
                value = value + factor[i, k] * inverse[k, j]
            inverse[i, j] = -value / factor[i, i]
    zero = jnp.zeros_like(factor[0, 0])

    def upper(i, j):
        return factor.get((i, j), zero)

    hess = [[upper(i, k) * shifts[k] + upper(i, k + 1) * (1.0 / growth) for k in range(steps)] for i in range(order)]
    target = [upper(i, 0) for i in range(order)]
    for k in range(steps):
        top, below = hess[k][k], hess[k + 1][k]
        radius = jnp.sqrt(top * top + below * below)
        cosine, sine = top / radius, below / radius
        for c in range(k, steps):
            a, b = hess[k][c], hess[k + 1][c]
            hess[k][c] = cosine * a + sine * b
            hess[k + 1][c] = cosine * b - sine * a
        a, b = target[k], target[k + 1]
        target[k] = cosine * a + sine * b
        target[k + 1] = cosine * b - sine * a
    weights = [None] * steps
    for i in range(steps - 1, -1, -1):
        value = target[i]
        for k in range(i + 1, steps):
            value = value - hess[i][k] * weights[k]
        weights[i] = value / hess[i][i]
    combine = []
    for j in range(order):
        value = zero + (1.0 if j == 0 else 0.0)
        if j < steps:
            value = value - shifts[j] * weights[j]
        if j > 0:
            value = value - (1.0 / growth) * weights[j - 1]
        combine.append(value)
    return factor, inverse, weights, combine


def combine_kernel(cells, gram, v, w, basis, factor_out, solution_out, residual, table, basis_v, sol_v, res_v, factor_v, sem, factor_sem):
    order, nx, ny, nz = basis_v.shape
    steps = order - 1
    pairs = [(j, k) for k in range(order) for j in range(k + 1)]
    tail = len(pairs)

    factor, inverse, weights, combine = small_algebra(gram[...], steps, cells)
    values = [inverse[p] for p in pairs] + weights + combine
    for n, value in enumerate(values):
        table[n] = jnp.broadcast_to(value, table.shape[1:])
    row = lax.broadcasted_iota(jnp.int32, (8, ROWS), 0)
    column = lax.broadcasted_iota(jnp.int32, (8, ROWS), 1)
    whole = jnp.zeros((8, ROWS), jnp.float32)
    for (i, j), value in factor.items():
        whole = jnp.where((row == i) & (column == j), value, whole)
    factor_v[...] = whole[:order, :order]
    factor_copy = pltpu.make_async_copy(factor_v, factor_out, factor_sem)
    factor_copy.start()

    def mul(n, x):
        return table[n][None] * x

    deep = 16 if ny % 16 == 0 else 8

    def tile(p, t):
        rows = pl.ds(pl.multiple_of(t * deep, deep), deep)
        for q in range(0, nz, ROWS):
            lanes = slice(q, q + ROWS)
            load = lambda x: x.reshape(deep // 8, 8, ROWS)
            padded = pl.ds(pl.multiple_of(PAD + t * deep, 8), deep)
            fields = [load(v[k, p, padded, lanes]) for k in range(order)]
            for k in range(order):
                total = None
                for j in range(k + 1):
                    term = mul(pairs.index((j, k)), fields[j])
                    total = term if total is None else total + term
                basis_v[k, p, rows, lanes] = total.reshape(deep, ROWS)
            total = mul(tail, load(w[0, p, padded, lanes]))
            for k in range(1, steps):
                total = total + mul(tail + k, load(w[k, p, padded, lanes]))
            sol_v[p, rows, lanes] = total.reshape(deep, ROWS)
            total = mul(tail + steps, fields[0])
            for j in range(1, order):
                total = total + mul(tail + steps + j, fields[j])
            res_v[p, rows, lanes] = total.reshape(deep, ROWS)

    def copies(p):
        return (
            pltpu.make_async_copy(basis_v.at[:, p], basis.at[:, p], sem.at[p, 0]),
            pltpu.make_async_copy(sol_v.at[p], solution_out.at[p], sem.at[p, 1]),
            pltpu.make_async_copy(res_v.at[p], residual.at[p], sem.at[p, 2]),
        )

    def plane(p, c):
        def inner(t, d):
            tile(p, t)
            return d

        lax.fori_loop(0, ny // deep, inner, 0)
        for copy in copies(p):
            copy.start()
        return c

    def finish(p, c):
        for copy in copies(p):
            copy.wait()
        return c

    lax.fori_loop(0, nx, plane, 0)
    lax.fori_loop(0, nx, finish, 0)
    factor_copy.wait()


def device_body(n_gx, n_gy, rhs, coefs, shifts):
    steps = shifts.shape[0]
    order = steps + 1
    nx, ny, nz = rhs.shape
    f32 = jnp.float32
    grown = (nx, ny + 2 * PAD, nz)
    height = -(-(order * (order + 1) // 2) // 8) * 8
    gram_rows = height + -(-steps // 8) * 8
    tiles = ny // TILE
    hbm = pl.BlockSpec(memory_space=pltpu.HBM)
    vmem = pl.BlockSpec(memory_space=pltpu.VMEM)
    dma = pltpu.SemaphoreType.DMA
    rhs = pltpu.with_memory_space_constraint(rhs, pltpu.HBM)
    coefs = pltpu.with_memory_space_constraint(coefs, pltpu.HBM)
    shifts = pltpu.with_memory_space_constraint(shifts, pltpu.HBM)
    v, w, gram = pl.pallas_call(
        functools.partial(basis_kernel, n_gx, n_gy),
        out_shape=(
            jax.ShapeDtypeStruct((order,) + grown, f32),
            jax.ShapeDtypeStruct((steps,) + grown, f32),
            jax.ShapeDtypeStruct((gram_rows, ROWS), f32),
        ),
        in_specs=[hbm, hbm, hbm],
        out_specs=(vmem, vmem, vmem),
        scratch_shapes=[
            pltpu.VMEM(coefs.shape, f32),
            pltpu.VMEM((height, ROWS), f32),
            pltpu.VMEM((order, 8, nz), f32),
            pltpu.VMEM((n_gx * n_gy, ROWS), f32),
            pltpu.SMEM(shifts.shape, f32),
            pltpu.VMEM((order, 2, 2, ny, nz), f32),
            pltpu.VMEM((steps, 2, 2, ny, nz), f32),
            pltpu.VMEM((order, 2, 2, nx, nz), f32),
            pltpu.VMEM((steps, 2, 2, nx, nz), f32),
            pltpu.VMEM((4 * order, 1, nz), f32),
            pltpu.VMEM((4 * steps, 1, nz), f32),
            pltpu.VMEM((2, ny, nz), f32),
            pltpu.VMEM((2, 2, nz), f32),
            pltpu.VMEM((2, nx, nz), f32),
            pltpu.VMEM((2, 2, nz), f32),
            pltpu.VMEM((2, nx, nz), f32),
            pltpu.VMEM((2, 2, nz), f32),
            pltpu.VMEM((2, 2, nz), f32),
            dma((6,)),
            pltpu.SemaphoreType.REGULAR((16,)),
            dma((2 * steps * tiles,)),
            dma((2 * steps * tiles,)),
            dma((2 * steps,)),
            dma((2 * steps,)),
            dma((4 * steps,)),
            dma((4 * steps,)),
            dma((2, 2 * tiles + 3)),
            dma((2, 2 * tiles + 3)),
            dma((1,)),
            dma((1,)),
        ],
        compiler_params=pltpu.CompilerParams(
            collective_id=0, has_side_effects=True, vmem_limit_bytes=32 * 2**20
        ),
        name="basis",
    )(shifts, rhs, coefs)

    cells = float(nx * ny * nz * n_gx * n_gy)
    return pl.pallas_call(
        functools.partial(combine_kernel, cells),
        out_shape=(
            jax.ShapeDtypeStruct((order, nx, ny, nz), f32),
            jax.ShapeDtypeStruct((order, order), f32),
            jax.ShapeDtypeStruct((nx, ny, nz), f32),
            jax.ShapeDtypeStruct((nx, ny, nz), f32),
        ),
        in_specs=[vmem, vmem, vmem],
        out_specs=(hbm, hbm, hbm, hbm),
        scratch_shapes=[
            pltpu.VMEM((order * (order + 1) // 2 + steps + order, 8, ROWS), f32),
            pltpu.VMEM((order, nx, ny, nz), f32),
            pltpu.VMEM((nx, ny, nz), f32),
            pltpu.VMEM((nx, ny, nz), f32),
            pltpu.VMEM((order, order), f32),
            dma((nx, 3)),
            dma,
        ],
        compiler_params=pltpu.CompilerParams(vmem_limit_bytes=32 * 2**20),
        name="combine",
    )(gram, v, w)


def solution(mesh):
    placed = (P("gx", "gy", None), P(None, "gx", "gy", None), P())
    return jax.shard_map(
        functools.partial(device_body, mesh.shape["gx"], mesh.shape["gy"]),
        mesh=mesh,
        in_specs=placed,
        out_specs=(P(None, "gx", "gy", None), P(), P("gx", "gy", None), P("gx", "gy", None)),
        check_vma=False,
    )
```
